128 devices in a mesh: sect: 4 (over x), space: 32 (over z, y, core).
Axes of the slice: x: 4, y: 4, z: 4, core: 2. Of those that a mesh axis runs over, the one named last changes fastest.
Arguments:
- dist: bfloat16 [8000, 65536], P('sect', 'space'), may hold values from 0.25 to 4
- velocity: float32 [3, 8000], P(None, 'sect'), may hold values from -1.5 to 1.5
- quad_weight: float32 [8000], P('sect'), may hold values from 0.5 to 2
- collision_rate: float32 [65536], P('space'), may hold values from 0.1 to 0.9
- ghost_source: int32 [8192], P('space'), may hold values from 0 to 2047
- ghost_owner: int32 [8192, 1], P('space'), may hold values from 0 to 31; in each aligned block of 256 rows (0 to 255, 256 to 511, ...) at most 16 rows name the same one
- wall_cell: int32 [32, 32, 16], P('space'), may hold values from 0 to 2047
- plenum_moments: float32 [16384, 20], P('space'), may hold values from -6 to 6
- iface_cell: int32 [16384], P('space'), may hold values from 0 to 65535, as said below
Outputs:
- relaxed: bfloat16 [8000, 65536], P('sect', 'space')
The draws below stay inside these ranges and needn't reach their ends.
Inputs may be any that keep to these rules, and one draw needn't show every extreme that they name: `ghost_owner`: in the rows of one slab no owner is named more than 16 times, a bound that some block reaches. `iface_cell`: distinct gap cells.
All inputs are finite; a program needn't handle non-finite values.
Results may differ from the reference program's by a relative error of at most 0.0065.
Values may be sent and summed in bfloat16 or wider, within the bound.
A program may use at most 192 MiB of HBM per device.

```python
import math
import jax
import jax.numpy as jnp
import numpy as np
from jax import lax

NV = 8000
MOMENTS = 20
CELL_DEV = 2048
GH_DEV = 256
NC = 65536
GHOST = 8192
CAP = 16
IFACE = 16384
N_SECT = 4
N_SPACE = 32


def draw_iface_cell(key, part):
    order = jax.random.permutation(key, NC)
    return order[:IFACE].astype(jnp.int32)


def plant(values, rng, smallest, largest):
    index_at = [jax.random.randint(jax.random.fold_in(rng, axis), (), 0, length) for axis, length in enumerate(values.shape)]
    widest = values.shape.index(max(values.shape))
    next_to = index_at[:widest] + [(index_at[widest] + 1) % values.shape[widest]] + index_at[widest + 1:]
    return values.at[tuple(index_at)].set(smallest).at[tuple(next_to)].set(largest)


def steps_of(stream_key, shape, cuts, smallest, top_value):
    loudness = 1.0
    for dim, shards_of in cuts:
        draws = jax.random.uniform(jax.random.fold_in(jax.random.fold_in(stream_key, 6), dim), (shards_of,), jnp.float32, smallest / len(cuts), top_value / len(cuts))
        loudness = loudness * jnp.repeat(jnp.exp(draws), shape[dim] // shards_of).reshape((-1,) + (1,) * (len(shape) - 1 - dim))
    return loudness


def assign_block(own_key, own, number, rows, amount, top, reach, skew):
    ranking = jax.random.permutation(own_key, amount)
    packed, common = portions_of(amount, rows * top, reach, skew, True), portions_of(amount, rows * top, reach, skew, False)
    places = jnp.arange(amount)

    def named(lengths, offset_by):
        used = int((lengths > 0).sum())
        fixed = max(1, used // 4)
        passed = fixed + (places - fixed + offset_by * (used - fixed)) % max(1, amount - fixed)
        return jnp.zeros((amount,), jnp.int32).at[ranking[jnp.where(places < fixed, places, passed)]].set(jnp.asarray(lengths, jnp.int32))

    lengths = jnp.where(number % 4 == 0, named(packed, number // 4), named(common, number - number // 4 - 1))
    mixed = jax.random.permutation(jax.random.fold_in(own, 3), amount)
    donor, taker = mixed[0:amount // 2 * 2:2], mixed[1:amount // 2 * 2:2]
    room = jnp.minimum(lengths[donor] - 1, reach - lengths[taker]) // 2
    room = jnp.where((donor == ranking[0]) | (taker == ranking[0]) | (lengths[taker] == 0), 0, jnp.maximum(room, 0))
    passed = jax.random.randint(jax.random.fold_in(own, 4), (amount // 2,), 0, 1 << 20) % (room + 1)
    lengths = lengths.at[donor].add(-passed).at[taker].add(passed)
    members = jnp.searchsorted(jnp.cumsum(lengths), jnp.arange(rows * top), side="right").astype(jnp.int32)
    grid = members.reshape(top, rows).T
    grid = grid[jax.random.permutation(jax.random.fold_in(own, 1), rows)]
    offset_by = jax.random.randint(jax.random.fold_in(own, 2), (rows, 1), 0, top)
    return jnp.take_along_axis(grid, (jnp.arange(top)[None, :] + offset_by) % top, axis=1)


def portions_of(amount, total, limit, skew, full):
    loads = [(1 << 20) // math.isqrt(grade ** skew) + 1 for grade in range(1, amount + 1)]
    largest = limit if full else min(limit, max(-(-total // amount), total * loads[0] // sum(loads)))
    least = 1 if total - largest >= amount - 1 else 0
    holding, spare = [largest] + [least] * (amount - 1), total - largest - least * (amount - 1)
    while spare > 0:
        movable = [i for i in range(1, amount) if holding[i] < largest] or [i for i in range(1, amount) if holding[i] < limit]
        pool, left = sum([loads[i] for i in movable]), spare
        for i in movable:
            more = min(limit - holding[i], max(1, left * loads[i] // pool), spare)
            holding[i] = holding[i] + more
            spare = spare - more
    return np.array(holding)


def bell_draw(key, dims, deviation, reach, pieces=(), held_as=jnp.bfloat16):
    entries = deviation * jax.random.normal(key, dims, jnp.float32)
    if pieces:
        entries = entries * steps_of(key, dims, pieces, -0.22, 0.18)
    return jnp.clip(entries, -reach, reach).astype(held_as)


def setup_inputs(seed: int = 0) -> dict:
    splits = jax.random.split(jax.random.key(seed), 10)
    dist = jnp.clip(jnp.exp(math.log(4.0) - 2.7725887 * jax.random.uniform(splits[0], (NV, NC), jnp.float32) ** steps_of(splits[0], (NV, NC), ((0, 4), (1, 32)), -0.2, 0.2)), 0.25, 4.0).astype(jnp.bfloat16)
    velocity = jnp.clip(jax.random.uniform(splits[1], (3, NV), jnp.float32, -1.5, 1.5) * steps_of(splits[1], (3, NV), ((1, 4),), -0.4, 0.0), -1.5, 1.5)
    quad_weight = jnp.clip(jnp.exp(math.log(2.0) - 1.3862944 * jax.random.uniform(splits[2], (NV,), jnp.float32) ** steps_of(splits[2], (NV,), ((0, 4),), -0.2, 0.2)), 0.5, 2.0)
    collision_rate = jnp.clip(jnp.exp(math.log(0.9) - 2.1972245 * jax.random.uniform(splits[3], (NC,), jnp.float32) ** steps_of(splits[3], (NC,), ((0, 32),), -0.2, 0.2)), 0.1, 0.9)
    ghost_source = plant(jax.random.randint(splits[4], (GHOST,), 0, CELL_DEV), jax.random.fold_in(splits[4], 1), 0, CELL_DEV - 1).astype(jnp.int32)
    ghost_owner_keys = jax.random.split(jax.random.fold_in(splits[5], 1), GHOST // GH_DEV)
    ghost_owner_turns = jax.random.permutation(jax.random.fold_in(splits[5], 3), GHOST // GH_DEV)
    ghost_owner = jax.vmap(lambda own, number: assign_block(jax.random.fold_in(splits[5], 2), own, number, GH_DEV, N_SPACE, 1, CAP, 2))(ghost_owner_keys, ghost_owner_turns).reshape((GHOST, 1))
    wall_cell = plant(jax.random.randint(splits[6], (N_SPACE, N_SPACE, CAP), 0, CELL_DEV), jax.random.fold_in(splits[6], 1), 0, CELL_DEV - 1).astype(jnp.int32)
    plenum_moments = bell_draw(splits[7], (IFACE, MOMENTS), 1.0, 6.0, ((0, 32),), jnp.float32)
    iface_cell = draw_iface_cell(jax.random.fold_in(splits[9], 71), 0)
    return dict(dist=dist, velocity=velocity, quad_weight=quad_weight, collision_rate=collision_rate, ghost_source=ghost_source, ghost_owner=ghost_owner, wall_cell=wall_cell, plenum_moments=plenum_moments, iface_cell=iface_cell)


COURANT_SCALE = 0.6
ES_SHIFT = -0.5
WALL_SHARE = 0.5
ORDER_TWO = ((0, 0), (1, 1), (2, 2), (0, 1), (0, 2), (1, 2))
ORDER_THREE = ((0, 0, 0), (1, 1, 1), (2, 2, 2), (0, 0, 1), (0, 0, 2), (1, 1, 0), (1, 1, 2), (2, 2, 0), (2, 2, 1), (0, 1, 2))
RECON_NORMS = (1.0, 1.0, 1.0, 1.0, 2.0, 2.0, 2.0, 1.0, 1.0, 1.0, 6.0, 6.0, 6.0, 2.0, 2.0, 2.0, 2.0, 2.0, 2.0, 1.0)


def hermite(velocity):
    unity_row = jnp.ones_like(velocity[0])
    stacked = [unity_row, velocity[0], velocity[1], velocity[2]]
    for (i, j) in ORDER_TWO:
        element = velocity[i] * velocity[j]
        if i == j:
            element = element - 1.0
        stacked.append(element)
    for (i, j, k) in ORDER_THREE:
        element = velocity[i] * velocity[j] * velocity[k]
        if i == j:
            element = element - velocity[k]
        if i == k:
            element = element - velocity[j]
        if j == k:
            element = element - velocity[i]
        stacked.append(element)
    return jnp.stack(stacked)


def moment_basis(velocity, weight):
    return (hermite(velocity) * (weight / NV)[None, :]).astype(jnp.bfloat16)


def recon_basis(velocity):
    norms = jnp.array(RECON_NORMS, dtype=jnp.float32)
    return (hermite(velocity) / norms[:, None]).T.astype(jnp.bfloat16)


def transport(padded, courant):
    left = padded[:, :-2].astype(jnp.float32)
    centre = padded[:, 1:-1].astype(jnp.float32)
    right = padded[:, 2:].astype(jnp.float32)
    ahead = jnp.maximum(courant, 0.0)
    behind = jnp.minimum(courant, 0.0)
    return (centre - ahead * (centre - left) - behind * (right - centre)).astype(jnp.bfloat16)


def es_targets(moments):
    density = moments[0]
    moving = [moments[1], moments[2], moments[3]]
    trace_sum = moments[4] + moments[5] + moments[6]
    second = [[None, None, None], [None, None, None], [None, None, None]]
    for n, (i, j) in enumerate(ORDER_TWO):
        element = (1.0 - ES_SHIFT) * moments[4 + n]
        if i == j:
            element = element + ES_SHIFT * trace_sum / 3.0
        second[i][j] = element
        second[j][i] = element
    stacked = [density] + moving + [second[i][j] for (i, j) in ORDER_TWO]
    for n, (i, j, k) in enumerate(ORDER_THREE):
        stacked.append(0.5 * moments[10 + n] + (moving[i] * second[j][k] + moving[j] * second[i][k] + moving[k] * second[i][j]) / density)
    return jnp.stack(stacked)


def slot_places(owner, peers, capacity):
    marks = (owner[:, None] == jnp.arange(peers, dtype=jnp.int32)[None, :]).astype(jnp.int32)
    before = jnp.cumsum(marks, axis=0) - marks
    slot = jnp.sum(marks * before, axis=1).astype(jnp.int32)
    return owner * capacity + slot


def reference(dist, velocity, quad_weight, collision_rate, ghost_source, ghost_owner, wall_cell, plenum_moments, iface_cell):
    block = NV // N_SECT
    dist_blocks = dist.reshape(N_SECT, block, NC)
    vel_blocks = velocity.reshape(3, N_SECT, block).transpose(1, 0, 2)
    weight_blocks = quad_weight.reshape(N_SECT, block)

    def read_of(piece, vel):
        courant = (COURANT_SCALE * vel[0])[:, None]
        padded = jnp.pad(piece, ((0, 0), (1, 1)))
        return transport(padded, courant)

    def accumulate(total, items):
        piece, vel, weight = items
        read = read_of(piece, vel)
        return total + jnp.dot(moment_basis(vel, weight), read, preferred_element_type=jnp.float32), None

    moments, unused = lax.scan(accumulate, jnp.zeros((MOMENTS, NC), jnp.float32), (dist_blocks, vel_blocks, weight_blocks))
    fluid = jnp.zeros((MOMENTS, NC), jnp.float32).at[:, iface_cell].set(plenum_moments.T)
    hit = jnp.zeros((NC,), jnp.float32).at[iface_cell].set(1.0)
    closure = es_targets(moments)
    targets = (closure + hit[None, :] * (fluid - closure)).astype(jnp.bfloat16)

    owner_grid = ghost_owner[:, 0].reshape(N_SPACE, GH_DEV).astype(jnp.int32)

    def places_of(owner):
        return slot_places(owner, N_SPACE, CAP)

    places = jax.vmap(places_of)(owner_grid)
    slot = (places - owner_grid * CAP).astype(jnp.int32)
    slab = jnp.arange(N_SPACE, dtype=jnp.int32)[:, None]
    source = (slab * CELL_DEV + ghost_source.reshape(N_SPACE, GH_DEV).astype(jnp.int32)).reshape(-1)
    landing = wall_cell[owner_grid, slab + 0 * owner_grid, slot].astype(jnp.int32)
    destination = (owner_grid * CELL_DEV + landing).reshape(-1)
    wall_moments = jnp.zeros((MOMENTS, NC), jnp.float32).at[:, destination].add(targets[:, source].astype(jnp.float32))
    rate = collision_rate[None, :]

    def relax(items):
        piece, vel = items
        read = read_of(piece, vel).astype(jnp.float32)
        recon = recon_basis(vel)
        equilibrium = jnp.dot(recon, targets, preferred_element_type=jnp.float32)
        wall_sum = jnp.dot(recon.astype(jnp.float32), wall_moments, precision=lax.Precision.HIGHEST)
        return (read + rate * (equilibrium - read) + WALL_SHARE * wall_sum).astype(jnp.bfloat16)

    relaxed = lax.map(relax, (dist_blocks, vel_blocks))
    return relaxed.reshape(NV, NC)
```

```python
import functools

import jax
import jax.numpy as jnp
from jax import lax
from jax.experimental import pallas as pl
from jax.experimental.pallas import tpu as pltpu
from jax.sharding import PartitionSpec as P

NV = 8000
MOMENTS = 20


COURANT_SCALE = 0.6
ES_SHIFT = -0.5
WALL_SHARE = 0.5
ORDER_TWO = ((0, 0), (1, 1), (2, 2), (0, 1), (0, 2), (1, 2))
ORDER_THREE = (
    (0, 0, 0),
    (1, 1, 1),
    (2, 2, 2),
    (0, 0, 1),
    (0, 0, 2),
    (1, 1, 0),
    (1, 1, 2),
    (2, 2, 0),
    (2, 2, 1),
    (0, 1, 2),
)
RECON_NORMS = (
    1.0,
    1.0,
    1.0,
    1.0,
    2.0,
    2.0,
    2.0,
    1.0,
    1.0,
    1.0,
    6.0,
    6.0,
    6.0,
    2.0,
    2.0,
    2.0,
    2.0,
    2.0,
    2.0,
    1.0,
)
ROW_BLOCK = 400
CELL_HI = 8


def halo_columns(shard):
    count = lax.axis_size("space")
    length = shard.shape[1]
    up = [(i, i + 1) for i in range(count - 1)]
    down = [(j, i) for i, j in up]
    before = lax.ppermute(shard[:, length - 1 :], "space", up)
    after = lax.ppermute(shard[:, :1], "space", down)
    return before, after


def hermite(velocity):
    unity_row = jnp.ones_like(velocity[0])
    stacked = [unity_row, velocity[0], velocity[1], velocity[2]]
    for i, j in ORDER_TWO:
        element = velocity[i] * velocity[j]
        if i == j:
            element = element - 1.0
        stacked.append(element)
    for i, j, k in ORDER_THREE:
        element = velocity[i] * velocity[j] * velocity[k]
        if i == j:
            element = element - velocity[k]
        if i == k:
            element = element - velocity[j]
        if j == k:
            element = element - velocity[i]
        stacked.append(element)
    return jnp.stack(stacked)


def moment_basis(velocity, weight):
    return (hermite(velocity) * (weight / NV)[None, :]).astype(jnp.bfloat16)


def recon_basis(velocity):
    norms = jnp.array(RECON_NORMS, dtype=jnp.float32)
    return (hermite(velocity) / norms[:, None]).T.astype(jnp.bfloat16)


def es_targets(moments):
    density = moments[0]
    moving = [moments[1], moments[2], moments[3]]
    trace_sum = moments[4] + moments[5] + moments[6]
    second = [[None, None, None], [None, None, None], [None, None, None]]
    for n, (i, j) in enumerate(ORDER_TWO):
        element = (1.0 - ES_SHIFT) * moments[4 + n]
        if i == j:
            element = element + ES_SHIFT * trace_sum / 3.0
        second[i][j] = element
        second[j][i] = element
    stacked = [density] + moving + [second[i][j] for i, j in ORDER_TWO]
    for n, (i, j, k) in enumerate(ORDER_THREE):
        stacked.append(
            0.5 * moments[10 + n]
            + (moving[i] * second[j][k] + moving[j] * second[i][k] + moving[k] * second[i][j])
            / density
        )
    return jnp.stack(stacked)


def transport_block(dist_ref, left_ref, right_ref, ahead_ref, behind_ref):
    centre = dist_ref[...].astype(jnp.float32)
    width = centre.shape[1]
    column = lax.broadcasted_iota(jnp.int32, centre.shape, 1)
    left = jnp.where(
        column == 0, left_ref[...].astype(jnp.float32), pltpu.roll(centre, 1, 1)
    )
    right = jnp.where(
        column == width - 1,
        right_ref[...].astype(jnp.float32),
        pltpu.roll(centre, width - 1, 1),
    )
    ahead = ahead_ref[...]
    behind = behind_ref[...]
    return (centre - ahead * (centre - left) - behind * (right - centre)).astype(jnp.bfloat16)


def moments_kernel(dist_ref, left_ref, right_ref, ahead_ref, behind_ref, basis_ref, out_ref):
    @pl.when(pl.program_id(0) == 0)
    def _():
        out_ref[...] = jnp.zeros_like(out_ref)

    read = transport_block(dist_ref, left_ref, right_ref, ahead_ref, behind_ref)
    out_ref[...] += jnp.dot(basis_ref[0], read, preferred_element_type=jnp.float32)


def relax_kernel(
    dist_ref, left_ref, right_ref, ahead_ref, behind_ref, recon_ref, recon3_ref, targets_ref,
    walls_ref, rate_ref, out_ref,
):
    read = transport_block(dist_ref, left_ref, right_ref, ahead_ref, behind_ref).astype(jnp.float32)
    equilibrium = jnp.dot(recon_ref[...], targets_ref[...], preferred_element_type=jnp.float32)
    wall_half = jnp.dot(recon3_ref[...], walls_ref[...], preferred_element_type=jnp.float32)
    rate = rate_ref[...]
    out_ref[...] = (read + rate * (equilibrium - read) + wall_half).astype(out_ref.dtype)


def row_spec(width):
    return pl.BlockSpec((ROW_BLOCK, width), lambda i: (i, 0))


def full_spec(shape):
    return pl.BlockSpec(shape, lambda i: (0,) * len(shape))


def moments_call(dist, left, right, ahead, behind, basis):
    rows, cells = dist.shape
    steps = rows // ROW_BLOCK
    blocks = basis.reshape(MOMENTS, steps, ROW_BLOCK).transpose(1, 0, 2)
    return pl.pallas_call(
        moments_kernel,
        grid=(steps,),
        in_specs=[
            row_spec(cells),
            row_spec(1),
            row_spec(1),
            row_spec(1),
            row_spec(1),
            pl.BlockSpec((1, MOMENTS, ROW_BLOCK), lambda i: (i, 0, 0)),
        ],
        out_specs=full_spec((MOMENTS, cells)),
        out_shape=jax.ShapeDtypeStruct((MOMENTS, cells), jnp.float32),
        compiler_params=pltpu.CompilerParams(dimension_semantics=("arbitrary",)),
        cost_estimate=pl.CostEstimate(
            flops=2 * rows * cells * MOMENTS + 8 * rows * cells,
            bytes_accessed=rows * cells * 2 + MOMENTS * cells * 4,
            transcendentals=0,
        ),
    )(dist, left, right, ahead, behind, blocks)


def relax_call(dist, left, right, ahead, behind, recon, recon3, targets, walls, rate):
    rows, cells = dist.shape
    steps = rows // ROW_BLOCK
    return pl.pallas_call(
        relax_kernel,
        grid=(steps,),
        in_specs=[
            row_spec(cells),
            row_spec(1),
            row_spec(1),
            row_spec(1),
            row_spec(1),
            row_spec(recon.shape[1]),
            row_spec(recon3.shape[1]),
            full_spec(targets.shape),
            full_spec(walls.shape),
            full_spec(rate.shape),
        ],
        out_specs=row_spec(cells),
        out_shape=jax.ShapeDtypeStruct((rows, cells), jnp.bfloat16),
        compiler_params=pltpu.CompilerParams(dimension_semantics=("parallel",)),
        cost_estimate=pl.CostEstimate(
            flops=2 * rows * cells * 80 + 12 * rows * cells,
            bytes_accessed=rows * cells * 4,
            transcendentals=0,
        ),
    )(dist, left, right, ahead, behind, recon, recon3, targets, walls, rate)


def split_three(values):
    first = values.astype(jnp.bfloat16)
    rest = values - first.astype(jnp.float32)
    second = rest.astype(jnp.bfloat16)
    third = (rest - second.astype(jnp.float32)).astype(jnp.bfloat16)
    return jnp.concatenate([first, second, third], axis=0)


def inject(closure, plenum_moments, iface_cell, base):
    width = closure.shape[1]
    low = width // CELL_HI
    coded = jnp.concatenate(
        [
            plenum_moments.astype(jnp.bfloat16),
            (iface_cell // 256).astype(jnp.bfloat16)[:, None],
            (iface_cell % 256).astype(jnp.bfloat16)[:, None],
        ],
        axis=1,
    )
    gathered = lax.all_gather(coded, "space", axis=0, tiled=True)
    rows = gathered[:, :MOMENTS]
    cells = gathered[:, MOMENTS].astype(jnp.int32) * 256 + gathered[:, MOMENTS + 1].astype(jnp.int32)
    local = cells - base
    valid = (local >= 0) & (local < width)
    upper = jnp.where(valid, local // low, -1)
    lower = local % low
    extended = jnp.concatenate([rows, jnp.ones((rows.shape[0], 1), jnp.bfloat16)], axis=1)
    pick_hi = (upper[:, None] == jnp.arange(CELL_HI, dtype=jnp.int32)[None, :]).astype(jnp.bfloat16)
    spread = (pick_hi[:, :, None] * extended[:, None, :]).reshape(rows.shape[0], -1)
    pick_lo = (lower[:, None] == jnp.arange(low, dtype=jnp.int32)[None, :]).astype(jnp.bfloat16)
    folded = lax.dot_general(
        spread, pick_lo, (((0,), (0,)), ((), ())), preferred_element_type=jnp.float32
    )
    folded = folded.reshape(CELL_HI, MOMENTS + 1, low).transpose(1, 0, 2).reshape(MOMENTS + 1, width)
    fluid = folded[:MOMENTS]
    hit = folded[MOMENTS]
    return closure + hit[None, :] * (fluid - closure)


def ghost_walls(targets, ghost_source, ghost_owner, wall_cell):
    cells = targets.shape[1]
    peers = lax.axis_size("space")
    capacity = wall_cell.shape[2]
    slots = peers * capacity
    owner = ghost_owner[:, 0]
    marks = (owner[:, None] == jnp.arange(peers, dtype=jnp.int32)[None, :]).astype(jnp.int32)
    before = jnp.cumsum(marks, axis=0) - marks
    slot = jnp.sum(marks * before, axis=1)
    places = owner * capacity + slot
    at_place = (places[:, None] == jnp.arange(slots, dtype=jnp.int32)[None, :]).astype(jnp.int32)
    source_of = jnp.sum(at_place * (ghost_source[:, None] + 1), axis=0) - 1
    select = (jnp.arange(cells, dtype=jnp.int32)[:, None] == source_of[None, :]).astype(jnp.bfloat16)
    outgoing = jnp.dot(targets, select, preferred_element_type=jnp.float32).astype(jnp.bfloat16)
    arrived = lax.all_to_all(outgoing, "space", split_axis=1, concat_axis=1, tiled=True)
    walls = wall_cell.reshape(slots)
    land = (walls[:, None] == jnp.arange(cells, dtype=jnp.int32)[None, :]).astype(jnp.bfloat16)
    return jnp.dot(arrived, land, preferred_element_type=jnp.float32)


def per_device(
    dist,
    velocity,
    quad_weight,
    collision_rate,
    ghost_source,
    ghost_owner,
    wall_cell,
    plenum_moments,
    iface_cell,
):
    cells = dist.shape[1]
    courant = COURANT_SCALE * velocity[0]
    ahead = jnp.maximum(courant, 0.0)[:, None]
    behind = jnp.minimum(courant, 0.0)[:, None]
    left, right = halo_columns(dist)
    partial_moments = moments_call(
        dist, left, right, ahead, behind, moment_basis(velocity, quad_weight)
    )
    slab_base = lax.axis_index("space") * cells
    moments = lax.psum(partial_moments, "sect")
    targets = inject(es_targets(moments), plenum_moments, iface_cell, slab_base).astype(
        jnp.bfloat16
    )
    wall_moments = ghost_walls(targets, ghost_source, ghost_owner, wall_cell)
    recon = recon_basis(velocity)
    recon3 = jnp.concatenate([recon, recon, recon], axis=1)
    walls = split_three(WALL_SHARE * wall_moments)
    return relax_call(
        dist, left, right, ahead, behind, recon, recon3, targets, walls, collision_rate[None, :]
    )


def solution(mesh):
    in_specs = (
        P("sect", "space"),
        P(None, "sect"),
        P("sect"),
        P("space"),
        P("space"),
        P("space", None),
        P("space", None, None),
        P("space", None),
        P("space"),
    )
    out_specs = P("sect", "space")
    return jax.shard_map(
        per_device, mesh=mesh, in_specs=in_specs, out_specs=out_specs, check_vma=False
    )
```

```python
import functools

import jax
import jax.numpy as jnp
from jax import lax
from jax.experimental import pallas as pl
from jax.experimental.pallas import tpu as pltpu
from jax.sharding import PartitionSpec as P

NV = 8000
MOMENTS = 20


COURANT_SCALE = 0.6
ES_SHIFT = -0.5
WALL_SHARE = 0.5
ORDER_TWO = ((0, 0), (1, 1), (2, 2), (0, 1), (0, 2), (1, 2))
ORDER_THREE = (
    (0, 0, 0),
    (1, 1, 1),
    (2, 2, 2),
    (0, 0, 1),
    (0, 0, 2),
    (1, 1, 0),
    (1, 1, 2),
    (2, 2, 0),
    (2, 2, 1),
    (0, 1, 2),
)
RECON_NORMS = (
    1.0,
    1.0,
    1.0,
    1.0,
    2.0,
    2.0,
    2.0,
    1.0,
    1.0,
    1.0,
    6.0,
    6.0,
    6.0,
    2.0,
    2.0,
    2.0,
    2.0,
    2.0,
    2.0,
    1.0,
)
ROW_BLOCK = 400
CELL_HI = 8


def halo_columns(shard):
    count = lax.axis_size("space")
    length = shard.shape[1]
    up = [(i, i + 1) for i in range(count - 1)]
    down = [(j, i) for i, j in up]
    before = lax.ppermute(shard[:, length - 1 :], "space", up)
    after = lax.ppermute(shard[:, :1], "space", down)
    return before, after


def hermite(velocity):
    unity_row = jnp.ones_like(velocity[0])
    stacked = [unity_row, velocity[0], velocity[1], velocity[2]]
    for i, j in ORDER_TWO:
        element = velocity[i] * velocity[j]
        if i == j:
            element = element - 1.0
        stacked.append(element)
    for i, j, k in ORDER_THREE:
        element = velocity[i] * velocity[j] * velocity[k]
        if i == j:
            element = element - velocity[k]
        if i == k:
            element = element - velocity[j]
        if j == k:
            element = element - velocity[i]
        stacked.append(element)
    return jnp.stack(stacked)


def moment_basis(velocity, weight):
    return (hermite(velocity) * (weight / NV)[None, :]).astype(jnp.bfloat16)


def recon_basis(velocity):
    norms = jnp.array(RECON_NORMS, dtype=jnp.float32)
    return (hermite(velocity) / norms[:, None]).T.astype(jnp.bfloat16)


def es_targets(moments):
    density = moments[0]
    moving = [moments[1], moments[2], moments[3]]
    trace_sum = moments[4] + moments[5] + moments[6]
    second = [[None, None, None], [None, None, None], [None, None, None]]
    for n, (i, j) in enumerate(ORDER_TWO):
        element = (1.0 - ES_SHIFT) * moments[4 + n]
        if i == j:
            element = element + ES_SHIFT * trace_sum / 3.0
        second[i][j] = element
        second[j][i] = element
    stacked = [density] + moving + [second[i][j] for i, j in ORDER_TWO]
    for n, (i, j, k) in enumerate(ORDER_THREE):
        stacked.append(
            0.5 * moments[10 + n]
            + (moving[i] * second[j][k] + moving[j] * second[i][k] + moving[k] * second[i][j])
            / density
        )
    return jnp.stack(stacked)


def transport_block(dist_ref, left_ref, right_ref, ahead_ref, behind_ref):
    centre = dist_ref[...].astype(jnp.float32)
    width = centre.shape[1]
    column = lax.broadcasted_iota(jnp.int32, centre.shape, 1)
    left = jnp.where(
        column == 0, left_ref[...].astype(jnp.float32), pltpu.roll(centre, 1, 1)
    )
    right = jnp.where(
        column == width - 1,
        right_ref[...].astype(jnp.float32),
        pltpu.roll(centre, width - 1, 1),
    )
    ahead = ahead_ref[...]
    behind = behind_ref[...]
    return (centre - ahead * (centre - left) - behind * (right - centre)).astype(jnp.bfloat16)


def moments_kernel(dist_ref, left_ref, right_ref, ahead_ref, behind_ref, basis_ref, out_ref):
    @pl.when(pl.program_id(0) == 0)
    def _():
        out_ref[...] = jnp.zeros_like(out_ref)

    read = transport_block(dist_ref, left_ref, right_ref, ahead_ref, behind_ref)
    out_ref[...] += jnp.dot(basis_ref[0], read, preferred_element_type=jnp.float32)


def relax_kernel(
    dist_ref, left_ref, right_ref, ahead_ref, behind_ref, recon_ref, recon3_ref, targets_ref,
    walls_ref, rate_ref, out_ref,
):
    read = transport_block(dist_ref, left_ref, right_ref, ahead_ref, behind_ref).astype(jnp.float32)
    equilibrium = jnp.dot(recon_ref[...], targets_ref[...], preferred_element_type=jnp.float32)
    wall_half = jnp.dot(recon3_ref[...], walls_ref[...], preferred_element_type=jnp.float32)
    rate = rate_ref[...]
    out_ref[...] = (read + rate * (equilibrium - read) + wall_half).astype(out_ref.dtype)


def row_spec(width):
    return pl.BlockSpec((ROW_BLOCK, width), lambda i: (i, 0))


def full_spec(shape):
    return pl.BlockSpec(shape, lambda i: (0,) * len(shape))


def moments_call(dist, left, right, ahead, behind, basis):
    rows, cells = dist.shape
    steps = rows // ROW_BLOCK
    blocks = basis.reshape(MOMENTS, steps, ROW_BLOCK).transpose(1, 0, 2)
    return pl.pallas_call(
        moments_kernel,
        grid=(steps,),
        in_specs=[
            row_spec(cells),
            row_spec(1),
            row_spec(1),
            row_spec(1),
            row_spec(1),
            pl.BlockSpec((1, MOMENTS, ROW_BLOCK), lambda i: (i, 0, 0)),
        ],
        out_specs=full_spec((MOMENTS, cells)),
        out_shape=jax.ShapeDtypeStruct((MOMENTS, cells), jnp.float32),
        compiler_params=pltpu.CompilerParams(dimension_semantics=("arbitrary",)),
        cost_estimate=pl.CostEstimate(
            flops=2 * rows * cells * MOMENTS + 8 * rows * cells,
            bytes_accessed=rows * cells * 2 + MOMENTS * cells * 4,
            transcendentals=0,
        ),
    )(dist, left, right, ahead, behind, blocks)


def relax_call(dist, left, right, ahead, behind, recon, recon3, targets, walls, rate):
    rows, cells = dist.shape
    steps = rows // ROW_BLOCK
    return pl.pallas_call(
        relax_kernel,
        grid=(steps,),
        in_specs=[
            row_spec(cells),
            row_spec(1),
            row_spec(1),
            row_spec(1),
            row_spec(1),
            row_spec(recon.shape[1]),
            row_spec(recon3.shape[1]),
            full_spec(targets.shape),
            full_spec(walls.shape),
            full_spec(rate.shape),
        ],
        out_specs=row_spec(cells),
        out_shape=jax.ShapeDtypeStruct((rows, cells), jnp.bfloat16),
        compiler_params=pltpu.CompilerParams(dimension_semantics=("parallel",)),
        cost_estimate=pl.CostEstimate(
            flops=2 * rows * cells * 80 + 12 * rows * cells,
            bytes_accessed=rows * cells * 4,
            transcendentals=0,
        ),
    )(dist, left, right, ahead, behind, recon, recon3, targets, walls, rate)


def split_three(values):
    first = values.astype(jnp.bfloat16)
    rest = values - first.astype(jnp.float32)
    second = rest.astype(jnp.bfloat16)
    third = (rest - second.astype(jnp.float32)).astype(jnp.bfloat16)
    return jnp.concatenate([first, second, third], axis=0)


def sect_sum(values):
    count = lax.axis_size("sect")
    total = values
    for shift in range(1, count):
        pairs = [(i, (i + shift) % count) for i in range(count)]
        total = total + lax.ppermute(values, "sect", pairs)
    return total


def interface_rows(plenum_moments, iface_cell, width, base):
    low = width // CELL_HI
    count = lax.axis_size("sect")
    share = plenum_moments.shape[0] // count
    start = lax.axis_index("sect") * share
    coded = jnp.concatenate(
        [
            plenum_moments.astype(jnp.bfloat16),
            (iface_cell // 256).astype(jnp.bfloat16)[:, None],
            (iface_cell % 256).astype(jnp.bfloat16)[:, None],
        ],
        axis=1,
    )
    coded = lax.dynamic_slice_in_dim(coded, start, share, axis=0)
    gathered = lax.all_gather(coded, "space", axis=0, tiled=True)
    rows = gathered[:, :MOMENTS]
    cells = gathered[:, MOMENTS].astype(jnp.int32) * 256 + gathered[:, MOMENTS + 1].astype(jnp.int32)
    local = cells - base
    valid = (local >= 0) & (local < width)
    upper = jnp.where(valid, local // low, -1)
    lower = local % low
    extended = jnp.concatenate([rows, jnp.ones((rows.shape[0], 1), jnp.bfloat16)], axis=1)
    pick_hi = (upper[:, None] == jnp.arange(CELL_HI, dtype=jnp.int32)[None, :]).astype(jnp.bfloat16)
    spread = (pick_hi[:, :, None] * extended[:, None, :]).reshape(rows.shape[0], -1)
    pick_lo = (lower[:, None] == jnp.arange(low, dtype=jnp.int32)[None, :]).astype(jnp.bfloat16)
    folded = lax.dot_general(
        spread, pick_lo, (((0,), (0,)), ((), ())), preferred_element_type=jnp.float32
    )
    return folded.reshape(CELL_HI, MOMENTS + 1, low).transpose(1, 0, 2).reshape(MOMENTS + 1, width)


def inject(closure, folded):
    fluid = folded[:MOMENTS]
    hit = folded[MOMENTS]
    return closure + hit[None, :] * (fluid - closure)


def ghost_walls(targets, ghost_source, ghost_owner, wall_cell):
    cells = targets.shape[1]
    peers = lax.axis_size("space")
    capacity = wall_cell.shape[2]
    slots = peers * capacity
    owner = ghost_owner[:, 0]
    marks = (owner[:, None] == jnp.arange(peers, dtype=jnp.int32)[None, :]).astype(jnp.int32)
    before = jnp.cumsum(marks, axis=0) - marks
    slot = jnp.sum(marks * before, axis=1)
    places = owner * capacity + slot
    at_place = (places[:, None] == jnp.arange(slots, dtype=jnp.int32)[None, :]).astype(jnp.int32)
    source_of = jnp.sum(at_place * (ghost_source[:, None] + 1), axis=0) - 1
    select = (jnp.arange(cells, dtype=jnp.int32)[:, None] == source_of[None, :]).astype(jnp.bfloat16)
    outgoing = jnp.dot(targets, select, preferred_element_type=jnp.float32).astype(jnp.bfloat16)
    arrived = lax.all_to_all(outgoing, "space", split_axis=1, concat_axis=1, tiled=True)
    walls = wall_cell.reshape(slots)
    land = (walls[:, None] == jnp.arange(cells, dtype=jnp.int32)[None, :]).astype(jnp.bfloat16)
    return jnp.dot(arrived, land, preferred_element_type=jnp.float32)


def per_device(
    dist,
    velocity,
    quad_weight,
    collision_rate,
    ghost_source,
    ghost_owner,
    wall_cell,
    plenum_moments,
    iface_cell,
):
    cells = dist.shape[1]
    courant = COURANT_SCALE * velocity[0]
    ahead = jnp.maximum(courant, 0.0)[:, None]
    behind = jnp.minimum(courant, 0.0)[:, None]
    left, right = halo_columns(dist)
    partial_moments = moments_call(
        dist, left, right, ahead, behind, moment_basis(velocity, quad_weight)
    )
    slab_base = lax.axis_index("space") * cells
    partial_rows = interface_rows(plenum_moments, iface_cell, cells, slab_base)
    summed = sect_sum(jnp.concatenate([partial_moments, partial_rows], axis=0))
    targets = inject(es_targets(summed[:MOMENTS]), summed[MOMENTS:]).astype(jnp.bfloat16)
    wall_moments = ghost_walls(targets, ghost_source, ghost_owner, wall_cell)
    recon = recon_basis(velocity)
    recon3 = jnp.concatenate([recon, recon, recon], axis=1)
    walls = split_three(WALL_SHARE * wall_moments)
    return relax_call(
        dist, left, right, ahead, behind, recon, recon3, targets, walls, collision_rate[None, :]
    )


def solution(mesh):
    in_specs = (
        P("sect", "space"),
        P(None, "sect"),
        P("sect"),
        P("space"),
        P("space"),
        P("space", None),
        P("space", None, None),
        P("space", None),
        P("space"),
    )
    out_specs = P("sect", "space")
    return jax.shard_map(
        per_device, mesh=mesh, in_specs=in_specs, out_specs=out_specs, check_vma=False
    )
```

```python
import jax
import jax.numpy as jnp
from jax import lax
from jax.experimental import pallas as pl
from jax.experimental.pallas import tpu as pltpu
from jax.sharding import PartitionSpec as P


NV = 8000
MOMENTS = 20


COURANT_SCALE = 0.6
ES_SHIFT = -0.5
WALL_SHARE = 0.5
ORDER_TWO = ((0, 0), (1, 1), (2, 2), (0, 1), (0, 2), (1, 2))
ORDER_THREE = (
    (0, 0, 0),
    (1, 1, 1),
    (2, 2, 2),
    (0, 0, 1),
    (0, 0, 2),
    (1, 1, 0),
    (1, 1, 2),
    (2, 2, 0),
    (2, 2, 1),
    (0, 1, 2),
)
RECON_NORMS = (
    1.0,
    1.0,
    1.0,
    1.0,
    2.0,
    2.0,
    2.0,
    1.0,
    1.0,
    1.0,
    6.0,
    6.0,
    6.0,
    2.0,
    2.0,
    2.0,
    2.0,
    2.0,
    2.0,
    1.0,
)
ROW_BLOCK = 400
CELL_HI = 8


def halo_columns(shard):
    count = lax.axis_size("space")
    length = shard.shape[1]
    up = [(i, i + 1) for i in range(count - 1)]
    down = [(j, i) for i, j in up]
    before = lax.ppermute(shard[:, length - 1 :], "space", up)
    after = lax.ppermute(shard[:, :1], "space", down)
    return before, after


def hermite(velocity):
    unity_row = jnp.ones_like(velocity[0])
    stacked = [unity_row, velocity[0], velocity[1], velocity[2]]
    for i, j in ORDER_TWO:
        element = velocity[i] * velocity[j]
        if i == j:
            element = element - 1.0
        stacked.append(element)
    for i, j, k in ORDER_THREE:
        element = velocity[i] * velocity[j] * velocity[k]
        if i == j:
            element = element - velocity[k]
        if i == k:
            element = element - velocity[j]
        if j == k:
            element = element - velocity[i]
        stacked.append(element)
    return jnp.stack(stacked)


def moment_basis(velocity, weight):
    return (hermite(velocity) * (weight / NV)[None, :]).astype(jnp.bfloat16)


def recon_basis(velocity):
    norms = jnp.array(RECON_NORMS, dtype=jnp.float32)
    return (hermite(velocity) / norms[:, None]).T.astype(jnp.bfloat16)


def es_targets(moments):
    density = moments[0]
    moving = [moments[1], moments[2], moments[3]]
    trace_sum = moments[4] + moments[5] + moments[6]
    second = [[None, None, None], [None, None, None], [None, None, None]]
    for n, (i, j) in enumerate(ORDER_TWO):
        element = (1.0 - ES_SHIFT) * moments[4 + n]
        if i == j:
            element = element + ES_SHIFT * trace_sum / 3.0
        second[i][j] = element
        second[j][i] = element
    stacked = [density] + moving + [second[i][j] for i, j in ORDER_TWO]
    for n, (i, j, k) in enumerate(ORDER_THREE):
        stacked.append(
            0.5 * moments[10 + n]
            + (moving[i] * second[j][k] + moving[j] * second[i][k] + moving[k] * second[i][j])
            / density
        )
    return jnp.stack(stacked)


def transport_block(dist_ref, left_ref, right_ref, ahead_ref, behind_ref):
    centre = dist_ref[...].astype(jnp.float32)
    width = centre.shape[1]
    column = lax.broadcasted_iota(jnp.int32, centre.shape, 1)
    left = jnp.where(
        column == 0, left_ref[...].astype(jnp.float32), pltpu.roll(centre, 1, 1)
    )
    right = jnp.where(
        column == width - 1,
        right_ref[...].astype(jnp.float32),
        pltpu.roll(centre, width - 1, 1),
    )
    ahead = ahead_ref[...]
    behind = behind_ref[...]
    return (centre - ahead * (centre - left) - behind * (right - centre)).astype(jnp.bfloat16)


def moments_kernel(dist_ref, left_ref, right_ref, ahead_ref, behind_ref, basis_ref, out_ref):
    @pl.when(pl.program_id(0) == 0)
    def _():
        out_ref[...] = jnp.zeros_like(out_ref)

    read = transport_block(dist_ref, left_ref, right_ref, ahead_ref, behind_ref)
    out_ref[...] += jnp.dot(basis_ref[0], read, preferred_element_type=jnp.float32)


def relax_kernel(
    dist_ref, left_ref, right_ref, ahead_ref, behind_ref, recon_ref, recon3_ref, targets_ref,
    walls_ref, rate_ref, out_ref,
):
    read = transport_block(dist_ref, left_ref, right_ref, ahead_ref, behind_ref).astype(jnp.float32)
    equilibrium = jnp.dot(recon_ref[...], targets_ref[...], preferred_element_type=jnp.float32)
    wall_half = jnp.dot(recon3_ref[...], walls_ref[...], preferred_element_type=jnp.float32)
    rate = rate_ref[...]
    out_ref[...] = (read + rate * (equilibrium - read) + wall_half).astype(out_ref.dtype)


def row_spec(width):
    return pl.BlockSpec((ROW_BLOCK, width), lambda i: (i, 0))


def full_spec(shape):
    return pl.BlockSpec(shape, lambda i: (0,) * len(shape))


def moments_call(dist, left, right, ahead, behind, basis):
    rows, cells = dist.shape
    steps = rows // ROW_BLOCK
    blocks = basis.reshape(MOMENTS, steps, ROW_BLOCK).transpose(1, 0, 2)
    return pl.pallas_call(
        moments_kernel,
        grid=(steps,),
        in_specs=[
            row_spec(cells),
            row_spec(1),
            row_spec(1),
            row_spec(1),
            row_spec(1),
            pl.BlockSpec((1, MOMENTS, ROW_BLOCK), lambda i: (i, 0, 0)),
        ],
        out_specs=full_spec((MOMENTS, cells)),
        out_shape=jax.ShapeDtypeStruct((MOMENTS, cells), jnp.float32),
        compiler_params=pltpu.CompilerParams(dimension_semantics=("arbitrary",)),
        cost_estimate=pl.CostEstimate(
            flops=2 * rows * cells * MOMENTS + 8 * rows * cells,
            bytes_accessed=rows * cells * 2 + MOMENTS * cells * 4,
            transcendentals=0,
        ),
    )(dist, left, right, ahead, behind, blocks)


def relax_call(dist, left, right, ahead, behind, recon, recon3, targets, walls, rate):
    rows, cells = dist.shape
    steps = rows // ROW_BLOCK
    return pl.pallas_call(
        relax_kernel,
        grid=(steps,),
        in_specs=[
            row_spec(cells),
            row_spec(1),
            row_spec(1),
            row_spec(1),
            row_spec(1),
            row_spec(recon.shape[1]),
            row_spec(recon3.shape[1]),
            full_spec(targets.shape),
            full_spec(walls.shape),
            full_spec(rate.shape),
        ],
        out_specs=row_spec(cells),
        out_shape=jax.ShapeDtypeStruct((rows, cells), jnp.bfloat16),
        compiler_params=pltpu.CompilerParams(dimension_semantics=("parallel",)),
        cost_estimate=pl.CostEstimate(
            flops=2 * rows * cells * 80 + 12 * rows * cells,
            bytes_accessed=rows * cells * 4,
            transcendentals=0,
        ),
    )(dist, left, right, ahead, behind, recon, recon3, targets, walls, rate)


def split_three(values):
    first = values.astype(jnp.bfloat16)
    rest = values - first.astype(jnp.float32)
    second = rest.astype(jnp.bfloat16)
    third = (rest - second.astype(jnp.float32)).astype(jnp.bfloat16)
    return jnp.concatenate([first, second, third], axis=0)


def sect_sum(values):
    count = lax.axis_size("sect")
    total = values
    for shift in range(1, count):
        pairs = [(i, (i + shift) % count) for i in range(count)]
        total = total + lax.ppermute(values, "sect", pairs)
    return total


def interface_rows(plenum_moments, iface_cell, width, base):
    count = lax.axis_size("sect")
    share = plenum_moments.shape[0] // count
    start = lax.axis_index("sect") * share
    coded = jnp.concatenate(
        [
            plenum_moments.astype(jnp.bfloat16),
            (iface_cell // 256).astype(jnp.bfloat16)[:, None],
            (iface_cell % 256).astype(jnp.bfloat16)[:, None],
        ],
        axis=1,
    )
    coded = lax.dynamic_slice_in_dim(coded, start, share, axis=0)
    peers = lax.axis_size("space")
    spread_out = jnp.broadcast_to(coded[None], (peers,) + coded.shape).reshape(peers * share, -1)
    gathered = lax.all_to_all(spread_out, "space", 0, 0, tiled=True)
    return fold_interface(gathered, width, base)


def fold_interface(gathered, width, base):
    low = width // CELL_HI
    rows = gathered[:, :MOMENTS]
    cells = gathered[:, MOMENTS].astype(jnp.int32) * 256 + gathered[:, MOMENTS + 1].astype(jnp.int32)
    local = cells - base
    valid = (local >= 0) & (local < width)
    upper = jnp.where(valid, local // low, -1)
    lower = local % low
    extended = jnp.concatenate([rows, jnp.ones((rows.shape[0], 1), jnp.bfloat16)], axis=1)
    pick_hi = (upper[:, None] == jnp.arange(CELL_HI, dtype=jnp.int32)[None, :]).astype(jnp.bfloat16)
    spread = (pick_hi[:, :, None] * extended[:, None, :]).reshape(rows.shape[0], -1)
    pick_lo = (lower[:, None] == jnp.arange(low, dtype=jnp.int32)[None, :]).astype(jnp.bfloat16)
    folded = lax.dot_general(
        spread, pick_lo, (((0,), (0,)), ((), ())), preferred_element_type=jnp.float32
    )
    return folded.reshape(CELL_HI, MOMENTS + 1, low).transpose(1, 0, 2).reshape(MOMENTS + 1, width)


def inject(closure, folded):
    fluid = folded[:MOMENTS]
    hit = folded[MOMENTS]
    return closure + hit[None, :] * (fluid - closure)


def ghost_walls(targets, ghost_source, ghost_owner, wall_cell):
    cells = targets.shape[1]
    peers = lax.axis_size("space")
    capacity = wall_cell.shape[2]
    slots = peers * capacity
    owner = ghost_owner[:, 0]
    marks = (owner[:, None] == jnp.arange(peers, dtype=jnp.int32)[None, :]).astype(jnp.int32)
    before = jnp.cumsum(marks, axis=0) - marks
    slot = jnp.sum(marks * before, axis=1)
    places = owner * capacity + slot
    at_place = (places[:, None] == jnp.arange(slots, dtype=jnp.int32)[None, :]).astype(jnp.int32)
    source_of = jnp.sum(at_place * (ghost_source[:, None] + 1), axis=0) - 1
    select = (jnp.arange(cells, dtype=jnp.int32)[:, None] == source_of[None, :]).astype(jnp.bfloat16)
    outgoing = jnp.dot(targets, select, preferred_element_type=jnp.float32).astype(jnp.bfloat16)
    arrived = lax.all_to_all(outgoing, "space", split_axis=1, concat_axis=1, tiled=True)
    walls = wall_cell.reshape(slots)
    land = (walls[:, None] == jnp.arange(cells, dtype=jnp.int32)[None, :]).astype(jnp.bfloat16)
    return jnp.dot(arrived, land, preferred_element_type=jnp.float32)


def per_device(
    dist,
    velocity,
    quad_weight,
    collision_rate,
    ghost_source,
    ghost_owner,
    wall_cell,
    plenum_moments,
    iface_cell,
):
    cells = dist.shape[1]
    courant = COURANT_SCALE * velocity[0]
    ahead = jnp.maximum(courant, 0.0)[:, None]
    behind = jnp.minimum(courant, 0.0)[:, None]
    left, right = halo_columns(dist)
    partial_moments = moments_call(
        dist, left, right, ahead, behind, moment_basis(velocity, quad_weight)
    )
    slab_base = lax.axis_index("space") * cells
    moments = sect_sum(partial_moments)
    partial_rows = interface_rows(plenum_moments, iface_cell, cells, slab_base)
    rows = sect_sum(partial_rows.astype(jnp.bfloat16)).astype(jnp.float32)
    targets = inject(es_targets(moments), rows).astype(jnp.bfloat16)
    wall_moments = ghost_walls(targets, ghost_source, ghost_owner, wall_cell)
    recon = recon_basis(velocity)
    recon3 = jnp.concatenate([recon, recon, recon], axis=1)
    walls = split_three(WALL_SHARE * wall_moments)
    return relax_call(
        dist, left, right, ahead, behind, recon, recon3, targets, walls, collision_rate[None, :]
    )


def solution(mesh):
    in_specs = (
        P("sect", "space"),
        P(None, "sect"),
        P("sect"),
        P("space"),
        P("space"),
        P("space", None),
        P("space", None, None),
        P("space", None),
        P("space"),
    )
    out_specs = P("sect", "space")

    return jax.shard_map(per_device, mesh=mesh, in_specs=in_specs, out_specs=out_specs, check_vma=False)
```

```python
import jax
import jax.numpy as jnp
from jax import lax
from jax.experimental import pallas as pl
from jax.experimental.pallas import tpu as pltpu
from jax.sharding import PartitionSpec as P


NV = 8000
MOMENTS = 20


COURANT_SCALE = 0.6
ES_SHIFT = -0.5
WALL_SHARE = 0.5
ORDER_TWO = ((0, 0), (1, 1), (2, 2), (0, 1), (0, 2), (1, 2))
ORDER_THREE = (
    (0, 0, 0),
    (1, 1, 1),
    (2, 2, 2),
    (0, 0, 1),
    (0, 0, 2),
    (1, 1, 0),
    (1, 1, 2),
    (2, 2, 0),
    (2, 2, 1),
    (0, 1, 2),
)
RECON_NORMS = (
    1.0,
    1.0,
    1.0,
    1.0,
    2.0,
    2.0,
    2.0,
    1.0,
    1.0,
    1.0,
    6.0,
    6.0,
    6.0,
    2.0,
    2.0,
    2.0,
    2.0,
    2.0,
    2.0,
    1.0,
)
ROW_BLOCK = 400
CELL_HI = 8


def halo_columns(shard):
    count = lax.axis_size("space")
    length = shard.shape[1]
    up = [(i, i + 1) for i in range(count - 1)]
    down = [(j, i) for i, j in up]
    before = lax.ppermute(shard[:, length - 1 :], "space", up)
    after = lax.ppermute(shard[:, :1], "space", down)
    return before, after


def hermite(velocity):
    unity_row = jnp.ones_like(velocity[0])
    stacked = [unity_row, velocity[0], velocity[1], velocity[2]]
    for i, j in ORDER_TWO:
        element = velocity[i] * velocity[j]
        if i == j:
            element = element - 1.0
        stacked.append(element)
    for i, j, k in ORDER_THREE:
        element = velocity[i] * velocity[j] * velocity[k]
        if i == j:
            element = element - velocity[k]
        if i == k:
            element = element - velocity[j]
        if j == k:
            element = element - velocity[i]
        stacked.append(element)
    return jnp.stack(stacked)


def moment_basis(velocity, weight):
    return (hermite(velocity) * (weight / NV)[None, :]).astype(jnp.bfloat16)


def recon_basis(velocity):
    norms = jnp.array(RECON_NORMS, dtype=jnp.float32)
    return (hermite(velocity) / norms[:, None]).T.astype(jnp.bfloat16)


def es_targets(moments):
    density = moments[0]
    moving = [moments[1], moments[2], moments[3]]
    trace_sum = moments[4] + moments[5] + moments[6]
    second = [[None, None, None], [None, None, None], [None, None, None]]
    for n, (i, j) in enumerate(ORDER_TWO):
        element = (1.0 - ES_SHIFT) * moments[4 + n]
        if i == j:
            element = element + ES_SHIFT * trace_sum / 3.0
        second[i][j] = element
        second[j][i] = element
    stacked = [density] + moving + [second[i][j] for i, j in ORDER_TWO]
    for n, (i, j, k) in enumerate(ORDER_THREE):
        stacked.append(
            0.5 * moments[10 + n]
            + (moving[i] * second[j][k] + moving[j] * second[i][k] + moving[k] * second[i][j])
            / density
        )
    return jnp.stack(stacked)


def transport_block(dist_ref, left_ref, right_ref, ahead_ref, behind_ref):
    centre = dist_ref[...].astype(jnp.float32)
    width = centre.shape[1]
    column = lax.broadcasted_iota(jnp.int32, (1, width), 1)
    left = jnp.where(
        column == 0, left_ref[...].astype(jnp.float32), pltpu.roll(centre, 1, 1)
    )
    right = jnp.where(
        column == width - 1,
        right_ref[...].astype(jnp.float32),
        pltpu.roll(centre, width - 1, 1),
    )
    ahead = ahead_ref[...]
    behind = behind_ref[...]
    return (centre - ahead * (centre - left) - behind * (right - centre)).astype(jnp.bfloat16)


def moments_kernel(dist_ref, left_ref, right_ref, ahead_ref, behind_ref, basis_ref, out_ref):
    @pl.when(pl.program_id(0) == 0)
    def _():
        out_ref[...] = jnp.zeros_like(out_ref)

    read = transport_block(dist_ref, left_ref, right_ref, ahead_ref, behind_ref)
    out_ref[...] += jnp.dot(basis_ref[0], read, preferred_element_type=jnp.float32)


def relax_kernel(
    dist_ref, left_ref, right_ref, ahead_ref, behind_ref, recon3_ref, gain_ref, keep_ref, out_ref,
):
    read = transport_block(dist_ref, left_ref, right_ref, ahead_ref, behind_ref).astype(jnp.float32)
    gained = jnp.dot(recon3_ref[...], gain_ref[...], preferred_element_type=jnp.float32)
    out_ref[...] = (read * keep_ref[...] + gained).astype(out_ref.dtype)


def row_spec(width):
    return pl.BlockSpec((ROW_BLOCK, width), lambda i: (i, 0))


def full_spec(shape):
    return pl.BlockSpec(shape, lambda i: (0,) * len(shape))


def moments_call(dist, left, right, ahead, behind, basis):
    rows, cells = dist.shape
    steps = rows // ROW_BLOCK
    blocks = basis.reshape(MOMENTS, steps, ROW_BLOCK).transpose(1, 0, 2)
    return pl.pallas_call(
        moments_kernel,
        grid=(steps,),
        in_specs=[
            row_spec(cells),
            row_spec(1),
            row_spec(1),
            row_spec(1),
            row_spec(1),
            pl.BlockSpec((1, MOMENTS, ROW_BLOCK), lambda i: (i, 0, 0)),
        ],
        out_specs=full_spec((MOMENTS, cells)),
        out_shape=jax.ShapeDtypeStruct((MOMENTS, cells), jnp.float32),
        compiler_params=pltpu.CompilerParams(dimension_semantics=("arbitrary",)),
        cost_estimate=pl.CostEstimate(
            flops=2 * rows * cells * MOMENTS + 8 * rows * cells,
            bytes_accessed=rows * cells * 2 + MOMENTS * cells * 4,
            transcendentals=0,
        ),
    )(dist, left, right, ahead, behind, blocks)


def relax_call(dist, left, right, ahead, behind, recon3, gain, keep):
    rows, cells = dist.shape
    steps = rows // ROW_BLOCK
    return pl.pallas_call(
        relax_kernel,
        grid=(steps,),
        in_specs=[
            row_spec(cells),
            row_spec(1),
            row_spec(1),
            row_spec(1),
            row_spec(1),
            row_spec(recon3.shape[1]),
            full_spec(gain.shape),
            full_spec(keep.shape),
        ],
        out_specs=row_spec(cells),
        out_shape=jax.ShapeDtypeStruct((rows, cells), jnp.bfloat16),
        compiler_params=pltpu.CompilerParams(dimension_semantics=("parallel",)),
        cost_estimate=pl.CostEstimate(
            flops=2 * rows * cells * 60 + 10 * rows * cells,
            bytes_accessed=rows * cells * 4,
            transcendentals=0,
        ),
    )(dist, left, right, ahead, behind, recon3, gain, keep)


def split_three(values):
    first = lax.reduce_precision(values, exponent_bits=8, mantissa_bits=7)
    rest = values - first
    second = lax.reduce_precision(rest, exponent_bits=8, mantissa_bits=7)
    third = rest - second
    parts = [first, second, third]
    return jnp.concatenate([part.astype(jnp.bfloat16) for part in parts], axis=0)


def sect_sum(values):
    count = lax.axis_size("sect")
    total = values
    for shift in range(1, count):
        pairs = [(i, (i + shift) % count) for i in range(count)]
        total = total + lax.ppermute(values, "sect", pairs)
    return total


def interface_rows(plenum_moments, iface_cell, width, base):
    count = lax.axis_size("sect")
    share = plenum_moments.shape[0] // count
    start = lax.axis_index("sect") * share
    coded = jnp.concatenate(
        [
            plenum_moments.astype(jnp.bfloat16),
            (iface_cell // 256).astype(jnp.bfloat16)[:, None],
            (iface_cell % 256).astype(jnp.bfloat16)[:, None],
        ],
        axis=1,
    )
    coded = lax.dynamic_slice_in_dim(coded, start, share, axis=0)
    peers = lax.axis_size("space")
    spread_out = jnp.broadcast_to(coded[None], (peers,) + coded.shape).reshape(peers * share, -1)
    gathered = lax.all_to_all(spread_out, "space", 0, 0, tiled=True)
    return fold_interface(gathered, width, base)


def fold_interface(gathered, width, base):
    low = width // CELL_HI
    rows = gathered[:, :MOMENTS]
    cells = gathered[:, MOMENTS].astype(jnp.int32) * 256 + gathered[:, MOMENTS + 1].astype(jnp.int32)
    local = cells - base
    valid = (local >= 0) & (local < width)
    upper = jnp.where(valid, local // low, -1)
    lower = local % low
    extended = jnp.concatenate([rows, jnp.ones((rows.shape[0], 1), jnp.bfloat16)], axis=1)
    pick_hi = (upper[:, None] == jnp.arange(CELL_HI, dtype=jnp.int32)[None, :]).astype(jnp.bfloat16)
    spread = (pick_hi[:, :, None] * extended[:, None, :]).reshape(rows.shape[0], -1)
    pick_lo = (lower[:, None] == jnp.arange(low, dtype=jnp.int32)[None, :]).astype(jnp.bfloat16)
    folded = lax.dot_general(
        spread, pick_lo, (((0,), (0,)), ((), ())), preferred_element_type=jnp.float32
    )
    return folded.reshape(CELL_HI, MOMENTS + 1, low).transpose(1, 0, 2).reshape(MOMENTS + 1, width)


def inject(closure, folded):
    fluid = folded[:MOMENTS]
    hit = folded[MOMENTS]
    return closure + hit[None, :] * (fluid - closure)


def ghost_walls(targets, ghost_source, ghost_owner, wall_cell):
    cells = targets.shape[1]
    peers = lax.axis_size("space")
    capacity = wall_cell.shape[2]
    slots = peers * capacity
    owner = ghost_owner[:, 0]
    marks = (owner[:, None] == jnp.arange(peers, dtype=jnp.int32)[None, :]).astype(jnp.int32)
    before = jnp.cumsum(marks, axis=0) - marks
    slot = jnp.sum(marks * before, axis=1)
    places = owner * capacity + slot
    at_place = (places[:, None] == jnp.arange(slots, dtype=jnp.int32)[None, :]).astype(jnp.int32)
    source_of = jnp.sum(at_place * (ghost_source[:, None] + 1), axis=0) - 1
    select = (jnp.arange(cells, dtype=jnp.int32)[:, None] == source_of[None, :]).astype(jnp.bfloat16)
    outgoing = jnp.dot(targets, select, preferred_element_type=jnp.float32).astype(jnp.bfloat16)
    arrived = lax.all_to_all(outgoing, "space", split_axis=1, concat_axis=1, tiled=True)
    walls = wall_cell.reshape(slots)
    land = (walls[:, None] == jnp.arange(cells, dtype=jnp.int32)[None, :]).astype(jnp.bfloat16)
    return jnp.dot(arrived, land, preferred_element_type=jnp.float32)


def per_device(
    dist,
    velocity,
    quad_weight,
    collision_rate,
    ghost_source,
    ghost_owner,
    wall_cell,
    plenum_moments,
    iface_cell,
):
    cells = dist.shape[1]
    courant = COURANT_SCALE * velocity[0]
    ahead = jnp.maximum(courant, 0.0)[:, None]
    behind = jnp.minimum(courant, 0.0)[:, None]
    left, right = halo_columns(dist)
    partial_moments = moments_call(
        dist, left, right, ahead, behind, moment_basis(velocity, quad_weight)
    )
    slab_base = lax.axis_index("space") * cells
    moments = sect_sum(partial_moments)
    partial_rows = interface_rows(plenum_moments, iface_cell, cells, slab_base)
    rows = sect_sum(partial_rows.astype(jnp.bfloat16)).astype(jnp.float32)
    targets = inject(es_targets(moments), rows).astype(jnp.bfloat16)
    wall_moments = ghost_walls(targets, ghost_source, ghost_owner, wall_cell)
    recon = recon_basis(velocity)
    recon3 = jnp.concatenate([recon, recon, recon], axis=1)
    rate = collision_rate[None, :]
    gain = split_three(rate * targets.astype(jnp.float32) + WALL_SHARE * wall_moments)
    return relax_call(dist, left, right, ahead, behind, recon3, gain, 1.0 - rate)


def solution(mesh):
    in_specs = (
        P("sect", "space"),
        P(None, "sect"),
        P("sect"),
        P("space"),
        P("space"),
        P("space", None),
        P("space", None, None),
        P("space", None),
        P("space"),
    )
    out_specs = P("sect", "space")

    return jax.shard_map(per_device, mesh=mesh, in_specs=in_specs, out_specs=out_specs, check_vma=False)
```

```python
import jax
import jax.numpy as jnp
from jax import lax
from jax.experimental import pallas as pl
from jax.experimental.pallas import tpu as pltpu
from jax.sharding import PartitionSpec as P


NV = 8000
MOMENTS = 20


COURANT_SCALE = 0.6
ES_SHIFT = -0.5
WALL_SHARE = 0.5
ORDER_TWO = ((0, 0), (1, 1), (2, 2), (0, 1), (0, 2), (1, 2))
ORDER_THREE = (
    (0, 0, 0),
    (1, 1, 1),
    (2, 2, 2),
    (0, 0, 1),
    (0, 0, 2),
    (1, 1, 0),
    (1, 1, 2),
    (2, 2, 0),
    (2, 2, 1),
    (0, 1, 2),
)
RECON_NORMS = (
    1.0,
    1.0,
    1.0,
    1.0,
    2.0,
    2.0,
    2.0,
    1.0,
    1.0,
    1.0,
    6.0,
    6.0,
    6.0,
    2.0,
    2.0,
    2.0,
    2.0,
    2.0,
    2.0,
    1.0,
)
ROW_BLOCK = 400
CELL_HI = 8


def halo_columns(shard):
    count = lax.axis_size("space")
    length = shard.shape[1]
    up = [(i, i + 1) for i in range(count - 1)]
    down = [(j, i) for i, j in up]
    before = lax.ppermute(shard[:, length - 1 :], "space", up)
    after = lax.ppermute(shard[:, :1], "space", down)
    return before, after


def hermite_tables():
    factors = [[0, 0, 0]]
    corrections = [[4, 4, 4]]
    for i in range(3):
        factors.append([i + 1, 0, 0])
        corrections.append([4, 4, 4])
    for i, j in ORDER_TWO:
        factors.append([i + 1, j + 1, 0])
        corrections.append([0 if i == j else 4, 4, 4])
    for i, j, k in ORDER_THREE:
        factors.append([i + 1, j + 1, k + 1])
        corrections.append(
            [k + 1 if i == j else 4, j + 1 if i == k else 4, i + 1 if j == k else 4]
        )
    return factors, corrections


def hermite(velocity):
    factors, corrections = hermite_tables()
    width = velocity.shape[1]
    extended = jnp.concatenate(
        [jnp.ones((1, width), jnp.float32), velocity, jnp.zeros((1, width), jnp.float32)], axis=0
    )
    rows = jnp.arange(5, dtype=jnp.int32)

    def pick(column):
        chosen = jnp.array(column, dtype=jnp.int32)
        select = (chosen[:, None] == rows[None, :]).astype(jnp.float32)
        return jnp.sum(select[:, :, None] * extended[None, :, :], axis=1)

    first, second, third = [pick([f[n] for f in factors]) for n in range(3)]
    element = first * second * third
    for n in range(3):
        element = element - pick([c[n] for c in corrections])
    return element


def moment_basis(velocity, weight):
    return (hermite(velocity) * (weight / NV)[None, :]).astype(jnp.bfloat16)


def recon_basis(velocity):
    norms = jnp.array(RECON_NORMS, dtype=jnp.float32)
    return (hermite(velocity) / norms[:, None]).T.astype(jnp.bfloat16)


def es_targets(moments):
    density = moments[0]
    moving = [moments[1], moments[2], moments[3]]
    trace_sum = moments[4] + moments[5] + moments[6]
    second = [[None, None, None], [None, None, None], [None, None, None]]
    for n, (i, j) in enumerate(ORDER_TWO):
        element = (1.0 - ES_SHIFT) * moments[4 + n]
        if i == j:
            element = element + ES_SHIFT * trace_sum / 3.0
        second[i][j] = element
        second[j][i] = element
    stacked = [density] + moving + [second[i][j] for i, j in ORDER_TWO]
    for n, (i, j, k) in enumerate(ORDER_THREE):
        stacked.append(
            0.5 * moments[10 + n]
            + (moving[i] * second[j][k] + moving[j] * second[i][k] + moving[k] * second[i][j])
            / density
        )
    return jnp.stack(stacked)


def transport_block(dist_ref, left_ref, right_ref, courant_ref):
    centre = dist_ref[...].astype(jnp.float32)
    width = centre.shape[1]
    column = lax.broadcasted_iota(jnp.int32, (1, width), 1)
    left = jnp.where(
        column == 0, left_ref[...].astype(jnp.float32), pltpu.roll(centre, 1, 1)
    )
    right = jnp.where(
        column == width - 1,
        right_ref[...].astype(jnp.float32),
        pltpu.roll(centre, width - 1, 1),
    )
    courant = courant_ref[...]
    ahead = jnp.maximum(courant, 0.0)
    behind = jnp.minimum(courant, 0.0)
    return (centre - ahead * (centre - left) - behind * (right - centre)).astype(jnp.bfloat16)


def moments_kernel(dist_ref, left_ref, right_ref, courant_ref, basis_ref, out_ref):
    @pl.when(pl.program_id(0) == 0)
    def _():
        out_ref[...] = jnp.zeros_like(out_ref)

    read = transport_block(dist_ref, left_ref, right_ref, courant_ref)
    out_ref[...] += jnp.dot(basis_ref[0], read, preferred_element_type=jnp.float32)


def relax_kernel(
    dist_ref, left_ref, right_ref, courant_ref, recon3_ref, gain_ref, keep_ref, out_ref,
):
    read = transport_block(dist_ref, left_ref, right_ref, courant_ref).astype(jnp.float32)
    gained = jnp.dot(recon3_ref[...], gain_ref[...], preferred_element_type=jnp.float32)
    out_ref[...] = (read * keep_ref[...] + gained).astype(out_ref.dtype)


def row_spec(width):
    return pl.BlockSpec((ROW_BLOCK, width), lambda i: (i, 0))


def full_spec(shape):
    return pl.BlockSpec(shape, lambda i: (0,) * len(shape))


def moments_call(dist, left, right, courant, basis):
    rows, cells = dist.shape
    steps = rows // ROW_BLOCK
    blocks = basis.reshape(MOMENTS, steps, ROW_BLOCK).transpose(1, 0, 2)
    return pl.pallas_call(
        moments_kernel,
        grid=(steps,),
        in_specs=[
            row_spec(cells),
            row_spec(1),
            row_spec(1),
            row_spec(1),
            pl.BlockSpec((1, MOMENTS, ROW_BLOCK), lambda i: (i, 0, 0)),
        ],
        out_specs=full_spec((MOMENTS, cells)),
        out_shape=jax.ShapeDtypeStruct((MOMENTS, cells), jnp.float32),
        compiler_params=pltpu.CompilerParams(dimension_semantics=("arbitrary",)),
        cost_estimate=pl.CostEstimate(
            flops=2 * rows * cells * MOMENTS + 8 * rows * cells,
            bytes_accessed=rows * cells * 2 + MOMENTS * cells * 4,
            transcendentals=0,
        ),
    )(dist, left, right, courant, blocks)


def relax_call(dist, left, right, courant, recon3, gain, keep):
    rows, cells = dist.shape
    steps = rows // ROW_BLOCK
    return pl.pallas_call(
        relax_kernel,
        grid=(steps,),
        in_specs=[
            row_spec(cells),
            row_spec(1),
            row_spec(1),
            row_spec(1),
            row_spec(recon3.shape[1]),
            full_spec(gain.shape),
            full_spec(keep.shape),
        ],
        out_specs=row_spec(cells),
        out_shape=jax.ShapeDtypeStruct((rows, cells), jnp.bfloat16),
        compiler_params=pltpu.CompilerParams(dimension_semantics=("parallel",)),
        cost_estimate=pl.CostEstimate(
            flops=2 * rows * cells * 60 + 10 * rows * cells,
            bytes_accessed=rows * cells * 4,
            transcendentals=0,
        ),
    )(dist, left, right, courant, recon3, gain, keep)


def split_three(values):
    first = lax.reduce_precision(values, exponent_bits=8, mantissa_bits=7)
    rest = values - first
    second = lax.reduce_precision(rest, exponent_bits=8, mantissa_bits=7)
    third = rest - second
    parts = [first, second, third]
    return jnp.concatenate([part.astype(jnp.bfloat16) for part in parts], axis=0)


def sect_sum(values):
    count = lax.axis_size("sect")
    total = values
    for shift in range(1, count):
        pairs = [(i, (i + shift) % count) for i in range(count)]
        total = total + lax.ppermute(values, "sect", pairs)
    return total


def interface_rows(plenum_moments, iface_cell, width, base):
    count = lax.axis_size("sect")
    share = plenum_moments.shape[0] // count
    start = lax.axis_index("sect") * share
    coded = jnp.concatenate(
        [
            plenum_moments.astype(jnp.bfloat16),
            (iface_cell // 256).astype(jnp.bfloat16)[:, None],
            (iface_cell % 256).astype(jnp.bfloat16)[:, None],
        ],
        axis=1,
    )
    coded = lax.dynamic_slice_in_dim(coded, start, share, axis=0)
    peers = lax.axis_size("space")
    spread_out = jnp.broadcast_to(coded[None], (peers,) + coded.shape).reshape(peers * share, -1)
    gathered = lax.all_to_all(spread_out, "space", 0, 0, tiled=True)
    return fold_interface(gathered, width, base)


def fold_interface(gathered, width, base):
    low = width // CELL_HI
    rows = gathered[:, :MOMENTS]
    cells = gathered[:, MOMENTS].astype(jnp.int32) * 256 + gathered[:, MOMENTS + 1].astype(jnp.int32)
    local = cells - base
    valid = (local >= 0) & (local < width)
    upper = jnp.where(valid, local // low, -1)
    lower = local % low
    extended = jnp.concatenate([rows, jnp.ones((rows.shape[0], 1), jnp.bfloat16)], axis=1)
    pick_hi = (upper[:, None] == jnp.arange(CELL_HI, dtype=jnp.int32)[None, :]).astype(jnp.bfloat16)
    spread = (pick_hi[:, :, None] * extended[:, None, :]).reshape(rows.shape[0], -1)
    pick_lo = (lower[:, None] == jnp.arange(low, dtype=jnp.int32)[None, :]).astype(jnp.bfloat16)
    folded = lax.dot_general(
        spread, pick_lo, (((0,), (0,)), ((), ())), preferred_element_type=jnp.float32
    )
    return folded.reshape(CELL_HI, MOMENTS + 1, low).transpose(1, 0, 2).reshape(MOMENTS + 1, width)


def inject(closure, folded):
    fluid = folded[:MOMENTS]
    hit = folded[MOMENTS]
    return closure + hit[None, :] * (fluid - closure)


def ghost_walls(targets, ghost_source, ghost_owner, wall_cell):
    cells = targets.shape[1]
    peers = lax.axis_size("space")
    capacity = wall_cell.shape[2]
    slots = peers * capacity
    owner = ghost_owner[:, 0]
    marks = (owner[:, None] == jnp.arange(peers, dtype=jnp.int32)[None, :]).astype(jnp.int32)
    before = jnp.cumsum(marks, axis=0) - marks
    slot = jnp.sum(marks * before, axis=1)
    places = owner * capacity + slot
    at_place = (places[:, None] == jnp.arange(slots, dtype=jnp.int32)[None, :]).astype(jnp.int32)
    source_of = jnp.sum(at_place * (ghost_source[:, None] + 1), axis=0) - 1
    select = (jnp.arange(cells, dtype=jnp.int32)[:, None] == source_of[None, :]).astype(jnp.bfloat16)
    outgoing = jnp.dot(targets, select, preferred_element_type=jnp.float32).astype(jnp.bfloat16)
    arrived = lax.all_to_all(outgoing, "space", split_axis=1, concat_axis=1, tiled=True)
    walls = wall_cell.reshape(slots)
    land = (walls[:, None] == jnp.arange(cells, dtype=jnp.int32)[None, :]).astype(jnp.bfloat16)
    return jnp.dot(arrived, land, preferred_element_type=jnp.float32)


def per_device(
    dist,
    velocity,
    quad_weight,
    collision_rate,
    ghost_source,
    ghost_owner,
    wall_cell,
    plenum_moments,
    iface_cell,
):
    cells = dist.shape[1]
    courant = (COURANT_SCALE * velocity[0])[:, None]
    left, right = halo_columns(dist)
    partial_moments = moments_call(
        dist, left, right, courant, moment_basis(velocity, quad_weight)
    )
    slab_base = lax.axis_index("space") * cells
    moments = sect_sum(partial_moments)
    partial_rows = interface_rows(plenum_moments, iface_cell, cells, slab_base)
    rows = sect_sum(partial_rows.astype(jnp.bfloat16)).astype(jnp.float32)
    targets = inject(es_targets(moments), rows).astype(jnp.bfloat16)
    wall_moments = ghost_walls(targets, ghost_source, ghost_owner, wall_cell)
    recon = recon_basis(velocity)
    recon3 = jnp.concatenate([recon, recon, recon], axis=1)
    rate = collision_rate[None, :]
    gain = split_three(rate * targets.astype(jnp.float32) + WALL_SHARE * wall_moments)
    return relax_call(dist, left, right, courant, recon3, gain, 1.0 - rate)


def solution(mesh):
    in_specs = (
        P("sect", "space"),
        P(None, "sect"),
        P("sect"),
        P("space"),
        P("space"),
        P("space", None),
        P("space", None, None),
        P("space", None),
        P("space"),
    )
    out_specs = P("sect", "space")

    return jax.shard_map(per_device, mesh=mesh, in_specs=in_specs, out_specs=out_specs, check_vma=False)
```

```python
import jax
import jax.numpy as jnp
from jax import lax
from jax.experimental import pallas as pl
from jax.experimental.pallas import tpu as pltpu
from jax.sharding import PartitionSpec as P


NV = 8000
MOMENTS = 20


COURANT_SCALE = 0.6
ES_SHIFT = -0.5
WALL_SHARE = 0.5
ORDER_TWO = ((0, 0), (1, 1), (2, 2), (0, 1), (0, 2), (1, 2))
ORDER_THREE = (
    (0, 0, 0),
    (1, 1, 1),
    (2, 2, 2),
    (0, 0, 1),
    (0, 0, 2),
    (1, 1, 0),
    (1, 1, 2),
    (2, 2, 0),
    (2, 2, 1),
    (0, 1, 2),
)
RECON_NORMS = (
    1.0,
    1.0,
    1.0,
    1.0,
    2.0,
    2.0,
    2.0,
    1.0,
    1.0,
    1.0,
    6.0,
    6.0,
    6.0,
    2.0,
    2.0,
    2.0,
    2.0,
    2.0,
    2.0,
    1.0,
)
ROW_BLOCK = 400
CELL_HI = 8


def halo_columns(shard):
    count = lax.axis_size("space")
    length = shard.shape[1]
    up = [(i, i + 1) for i in range(count - 1)]
    down = [(j, i) for i, j in up]
    before = lax.ppermute(shard[:, length - 1 :], "space", up)
    after = lax.ppermute(shard[:, :1], "space", down)
    return before, after


def hermite_tables():
    factors = [[0, 0, 0]]
    corrections = [[4, 4, 4]]
    for i in range(3):
        factors.append([i + 1, 0, 0])
        corrections.append([4, 4, 4])
    for i, j in ORDER_TWO:
        factors.append([i + 1, j + 1, 0])
        corrections.append([0 if i == j else 4, 4, 4])
    for i, j, k in ORDER_THREE:
        factors.append([i + 1, j + 1, k + 1])
        corrections.append(
            [k + 1 if i == j else 4, j + 1 if i == k else 4, i + 1 if j == k else 4]
        )
    return factors, corrections


def hermite(velocity):
    factors, corrections = hermite_tables()
    width = velocity.shape[1]
    extended = jnp.concatenate(
        [jnp.ones((1, width), jnp.float32), velocity, jnp.zeros((1, width), jnp.float32)], axis=0
    )
    rows = jnp.arange(5, dtype=jnp.int32)

    def pick(column):
        chosen = jnp.array(column, dtype=jnp.int32)
        select = (chosen[:, None] == rows[None, :]).astype(jnp.float32)
        return jnp.sum(select[:, :, None] * extended[None, :, :], axis=1)

    first, second, third = [pick([f[n] for f in factors]) for n in range(3)]
    element = first * second * third
    for n in range(3):
        element = element - pick([c[n] for c in corrections])
    return element


def moment_basis(velocity, weight):
    return (hermite(velocity) * (weight / NV)[None, :]).astype(jnp.bfloat16)


def recon_basis(velocity):
    norms = jnp.array(RECON_NORMS, dtype=jnp.float32)
    return (hermite(velocity) / norms[:, None]).T.astype(jnp.bfloat16)


def es_targets(moments):
    density = moments[0]
    moving = [moments[1], moments[2], moments[3]]
    trace_sum = moments[4] + moments[5] + moments[6]
    second = [[None, None, None], [None, None, None], [None, None, None]]
    for n, (i, j) in enumerate(ORDER_TWO):
        element = (1.0 - ES_SHIFT) * moments[4 + n]
        if i == j:
            element = element + ES_SHIFT * trace_sum / 3.0
        second[i][j] = element
        second[j][i] = element
    stacked = [density] + moving + [second[i][j] for i, j in ORDER_TWO]
    for n, (i, j, k) in enumerate(ORDER_THREE):
        stacked.append(
            0.5 * moments[10 + n]
            + (moving[i] * second[j][k] + moving[j] * second[i][k] + moving[k] * second[i][j])
            / density
        )
    return jnp.stack(stacked)


def transport_block(dist_ref, left_ref, right_ref, courant_ref):
    centre = dist_ref[...].astype(jnp.float32)
    width = centre.shape[1]
    column = lax.broadcasted_iota(jnp.int32, (1, width), 1)
    left = jnp.where(
        column == 0, left_ref[...].astype(jnp.float32), pltpu.roll(centre, 1, 1)
    )
    right = jnp.where(
        column == width - 1,
        right_ref[...].astype(jnp.float32),
        pltpu.roll(centre, width - 1, 1),
    )
    courant = courant_ref[...]
    ahead = jnp.maximum(courant, 0.0)
    behind = jnp.minimum(courant, 0.0)
    return (centre - ahead * (centre - left) - behind * (right - centre)).astype(jnp.bfloat16)


def moments_kernel(dist_ref, basis_ref, out_ref):
    @pl.when(pl.program_id(0) == 0)
    def _():
        out_ref[...] = jnp.zeros_like(out_ref)

    out_ref[...] += jnp.dot(basis_ref[0], dist_ref[...], preferred_element_type=jnp.float32)


def relax_kernel(
    dist_ref, left_ref, right_ref, courant_ref, recon3_ref, gain_ref, keep_ref, out_ref,
):
    read = transport_block(dist_ref, left_ref, right_ref, courant_ref).astype(jnp.float32)
    gained = jnp.dot(recon3_ref[...], gain_ref[...], preferred_element_type=jnp.float32)
    out_ref[...] = (read * keep_ref[...] + gained).astype(out_ref.dtype)


def row_spec(width):
    return pl.BlockSpec((ROW_BLOCK, width), lambda i: (i, 0))


def full_spec(shape):
    return pl.BlockSpec(shape, lambda i: (0,) * len(shape))


def moments_call(dist, basis):
    rows, cells = dist.shape
    steps = rows // ROW_BLOCK
    height = basis.shape[0]
    blocks = basis.reshape(height, steps, ROW_BLOCK).transpose(1, 0, 2)
    return pl.pallas_call(
        moments_kernel,
        grid=(steps,),
        in_specs=[
            row_spec(cells),
            pl.BlockSpec((1, height, ROW_BLOCK), lambda i: (i, 0, 0)),
        ],
        out_specs=full_spec((height, cells)),
        out_shape=jax.ShapeDtypeStruct((height, cells), jnp.float32),
        compiler_params=pltpu.CompilerParams(dimension_semantics=("arbitrary",)),
        cost_estimate=pl.CostEstimate(
            flops=2 * rows * cells * height,
            bytes_accessed=rows * cells * 2 + height * cells * 4,
            transcendentals=0,
        ),
    )(dist, blocks)


def stencil_moments(dist, left, right, courant, basis):
    ahead = jnp.maximum(courant[:, 0], 0.0)
    behind = jnp.minimum(courant[:, 0], 0.0)
    weights = basis.astype(jnp.float32)
    stencil = [weights * (1.0 - ahead + behind)[None, :], weights * ahead[None, :], -weights * behind[None, :]]
    stacked = split_three(jnp.concatenate(stencil, axis=0))
    products = moments_call(dist, stacked)
    parts = products.reshape(3, 3, MOMENTS, dist.shape[1])
    parts = (parts[0] + parts[1]) + parts[2]
    edge_left = jnp.sum(stencil[1] * left[:, 0].astype(jnp.float32)[None, :], axis=1)
    edge_right = jnp.sum(stencil[2] * right[:, 0].astype(jnp.float32)[None, :], axis=1)
    from_left = jnp.concatenate([edge_left[:, None], parts[1][:, :-1]], axis=1)
    from_right = jnp.concatenate([parts[2][:, 1:], edge_right[:, None]], axis=1)
    return (parts[0] + from_left) + from_right


def relax_call(dist, left, right, courant, recon3, gain, keep):
    rows, cells = dist.shape
    steps = rows // ROW_BLOCK
    return pl.pallas_call(
        relax_kernel,
        grid=(steps,),
        in_specs=[
            row_spec(cells),
            row_spec(1),
            row_spec(1),
            row_spec(1),
            row_spec(recon3.shape[1]),
            full_spec(gain.shape),
            full_spec(keep.shape),
        ],
        out_specs=row_spec(cells),
        out_shape=jax.ShapeDtypeStruct((rows, cells), jnp.bfloat16),
        compiler_params=pltpu.CompilerParams(dimension_semantics=("parallel",)),
        cost_estimate=pl.CostEstimate(
            flops=2 * rows * cells * 60 + 10 * rows * cells,
            bytes_accessed=rows * cells * 4,
            transcendentals=0,
        ),
    )(dist, left, right, courant, recon3, gain, keep)


def split_three(values):
    first = lax.reduce_precision(values, exponent_bits=8, mantissa_bits=7)
    rest = values - first
    second = lax.reduce_precision(rest, exponent_bits=8, mantissa_bits=7)
    third = rest - second
    parts = [first, second, third]
    return jnp.concatenate([part.astype(jnp.bfloat16) for part in parts], axis=0)


def sect_sum(values):
    count = lax.axis_size("sect")
    total = values
    for shift in range(1, count):
        pairs = [(i, (i + shift) % count) for i in range(count)]
        total = total + lax.ppermute(values, "sect", pairs)
    return total


def interface_rows(plenum_moments, iface_cell, width, base):
    count = lax.axis_size("sect")
    share = plenum_moments.shape[0] // count
    start = lax.axis_index("sect") * share
    coded = jnp.concatenate(
        [
            plenum_moments.astype(jnp.bfloat16),
            (iface_cell // 256).astype(jnp.bfloat16)[:, None],
            (iface_cell % 256).astype(jnp.bfloat16)[:, None],
        ],
        axis=1,
    )
    coded = lax.dynamic_slice_in_dim(coded, start, share, axis=0)
    peers = lax.axis_size("space")
    spread_out = jnp.broadcast_to(coded[None], (peers,) + coded.shape).reshape(peers * share, -1)
    gathered = lax.all_to_all(spread_out, "space", 0, 0, tiled=True)
    return fold_interface(gathered, width, base)


def fold_interface(gathered, width, base):
    low = width // CELL_HI
    rows = gathered[:, :MOMENTS]
    cells = gathered[:, MOMENTS].astype(jnp.int32) * 256 + gathered[:, MOMENTS + 1].astype(jnp.int32)
    local = cells - base
    valid = (local >= 0) & (local < width)
    upper = jnp.where(valid, local // low, -1)
    lower = local % low
    extended = jnp.concatenate([rows, jnp.ones((rows.shape[0], 1), jnp.bfloat16)], axis=1)
    pick_hi = (upper[:, None] == jnp.arange(CELL_HI, dtype=jnp.int32)[None, :]).astype(jnp.bfloat16)
    spread = (pick_hi[:, :, None] * extended[:, None, :]).reshape(rows.shape[0], -1)
    pick_lo = (lower[:, None] == jnp.arange(low, dtype=jnp.int32)[None, :]).astype(jnp.bfloat16)
    folded = lax.dot_general(
        spread, pick_lo, (((0,), (0,)), ((), ())), preferred_element_type=jnp.float32
    )
    return folded.reshape(CELL_HI, MOMENTS + 1, low).transpose(1, 0, 2).reshape(MOMENTS + 1, width)


def inject(closure, folded):
    fluid = folded[:MOMENTS]
    hit = folded[MOMENTS]
    return closure + hit[None, :] * (fluid - closure)


def ghost_walls(targets, ghost_source, ghost_owner, wall_cell):
    cells = targets.shape[1]
    peers = lax.axis_size("space")
    capacity = wall_cell.shape[2]
    slots = peers * capacity
    owner = ghost_owner[:, 0]
    marks = (owner[:, None] == jnp.arange(peers, dtype=jnp.int32)[None, :]).astype(jnp.int32)
    before = jnp.cumsum(marks, axis=0) - marks
    slot = jnp.sum(marks * before, axis=1)
    places = owner * capacity + slot
    at_place = (places[:, None] == jnp.arange(slots, dtype=jnp.int32)[None, :]).astype(jnp.int32)
    source_of = jnp.sum(at_place * (ghost_source[:, None] + 1), axis=0) - 1
    select = (jnp.arange(cells, dtype=jnp.int32)[:, None] == source_of[None, :]).astype(jnp.bfloat16)
    outgoing = jnp.dot(targets, select, preferred_element_type=jnp.float32).astype(jnp.bfloat16)
    arrived = lax.all_to_all(outgoing, "space", split_axis=1, concat_axis=1, tiled=True)
    walls = wall_cell.reshape(slots)
    land = (walls[:, None] == jnp.arange(cells, dtype=jnp.int32)[None, :]).astype(jnp.bfloat16)
    return jnp.dot(arrived, land, preferred_element_type=jnp.float32)


def per_device(
    dist,
    velocity,
    quad_weight,
    collision_rate,
    ghost_source,
    ghost_owner,
    wall_cell,
    plenum_moments,
    iface_cell,
):
    cells = dist.shape[1]
    courant = (COURANT_SCALE * velocity[0])[:, None]
    left, right = halo_columns(dist)
    partial_moments = stencil_moments(
        dist, left, right, courant, moment_basis(velocity, quad_weight)
    )
    slab_base = lax.axis_index("space") * cells
    moments = sect_sum(partial_moments)
    partial_rows = interface_rows(plenum_moments, iface_cell, cells, slab_base)
    rows = sect_sum(partial_rows.astype(jnp.bfloat16)).astype(jnp.float32)
    targets = inject(es_targets(moments), rows).astype(jnp.bfloat16)
    wall_moments = ghost_walls(targets, ghost_source, ghost_owner, wall_cell)
    recon = recon_basis(velocity)
    recon3 = jnp.concatenate([recon, recon, recon], axis=1)
    rate = collision_rate[None, :]
    gain = split_three(rate * targets.astype(jnp.float32) + WALL_SHARE * wall_moments)
    return relax_call(dist, left, right, courant, recon3, gain, 1.0 - rate)


def solution(mesh):
    in_specs = (
        P("sect", "space"),
        P(None, "sect"),
        P("sect"),
        P("space"),
        P("space"),
        P("space", None),
        P("space", None, None),
        P("space", None),
        P("space"),
    )
    out_specs = P("sect", "space")

    return jax.shard_map(per_device, mesh=mesh, in_specs=in_specs, out_specs=out_specs, check_vma=False)
```

```python
import jax
import jax.numpy as jnp
from jax import lax
from jax.experimental import pallas as pl
from jax.experimental.pallas import tpu as pltpu
from jax.sharding import PartitionSpec as P


NV = 8000
MOMENTS = 20


COURANT_SCALE = 0.6
ES_SHIFT = -0.5
WALL_SHARE = 0.5
ORDER_TWO = ((0, 0), (1, 1), (2, 2), (0, 1), (0, 2), (1, 2))
ORDER_THREE = (
    (0, 0, 0),
    (1, 1, 1),
    (2, 2, 2),
    (0, 0, 1),
    (0, 0, 2),
    (1, 1, 0),
    (1, 1, 2),
    (2, 2, 0),
    (2, 2, 1),
    (0, 1, 2),
)
RECON_NORMS = (
    1.0,
    1.0,
    1.0,
    1.0,
    2.0,
    2.0,
    2.0,
    1.0,
    1.0,
    1.0,
    6.0,
    6.0,
    6.0,
    2.0,
    2.0,
    2.0,
    2.0,
    2.0,
    2.0,
    1.0,
)
ROW_BLOCK = 400
CELL_HI = 8


def halo_columns(shard):
    count = lax.axis_size("space")
    length = shard.shape[1]
    up = [(i, i + 1) for i in range(count - 1)]
    down = [(j, i) for i, j in up]
    before = lax.ppermute(shard[:, length - 1 :], "space", up)
    after = lax.ppermute(shard[:, :1], "space", down)
    return before, after


def hermite_tables():
    factors = [[0, 0, 0]]
    corrections = [[4, 4, 4]]
    for i in range(3):
        factors.append([i + 1, 0, 0])
        corrections.append([4, 4, 4])
    for i, j in ORDER_TWO:
        factors.append([i + 1, j + 1, 0])
        corrections.append([0 if i == j else 4, 4, 4])
    for i, j, k in ORDER_THREE:
        factors.append([i + 1, j + 1, k + 1])
        corrections.append(
            [k + 1 if i == j else 4, j + 1 if i == k else 4, i + 1 if j == k else 4]
        )
    return factors, corrections


def hermite(velocity):
    factors, corrections = hermite_tables()
    width = velocity.shape[1]
    extended = jnp.concatenate(
        [jnp.ones((1, width), jnp.float32), velocity, jnp.zeros((1, width), jnp.float32)], axis=0
    )
    rows = jnp.arange(5, dtype=jnp.int32)

    def pick(column):
        chosen = jnp.array(column, dtype=jnp.int32)
        select = (chosen[:, None] == rows[None, :]).astype(jnp.float32)
        return jnp.sum(select[:, :, None] * extended[None, :, :], axis=1)

    first, second, third = [pick([f[n] for f in factors]) for n in range(3)]
    element = first * second * third
    for n in range(3):
        element = element - pick([c[n] for c in corrections])
    return element


def moment_basis(velocity, weight):
    return (hermite(velocity) * (weight / NV)[None, :]).astype(jnp.bfloat16)


def recon_basis(velocity):
    norms = jnp.array(RECON_NORMS, dtype=jnp.float32)
    return (hermite(velocity) / norms[:, None]).T.astype(jnp.bfloat16)


def es_targets(moments):
    density = moments[0]
    moving = [moments[1], moments[2], moments[3]]
    trace_sum = moments[4] + moments[5] + moments[6]
    second = [[None, None, None], [None, None, None], [None, None, None]]
    for n, (i, j) in enumerate(ORDER_TWO):
        element = (1.0 - ES_SHIFT) * moments[4 + n]
        if i == j:
            element = element + ES_SHIFT * trace_sum / 3.0
        second[i][j] = element
        second[j][i] = element
    stacked = [density] + moving + [second[i][j] for i, j in ORDER_TWO]
    for n, (i, j, k) in enumerate(ORDER_THREE):
        stacked.append(
            0.5 * moments[10 + n]
            + (moving[i] * second[j][k] + moving[j] * second[i][k] + moving[k] * second[i][j])
            / density
        )
    return jnp.stack(stacked)


def transport_block(dist_ref, left_ref, right_ref, courant_ref):
    centre = dist_ref[...].astype(jnp.float32)
    width = centre.shape[1]
    column = lax.broadcasted_iota(jnp.int32, (1, width), 1)
    left = jnp.where(
        column == 0, left_ref[...].astype(jnp.float32), pltpu.roll(centre, 1, 1)
    )
    right = jnp.where(
        column == width - 1,
        right_ref[...].astype(jnp.float32),
        pltpu.roll(centre, width - 1, 1),
    )
    courant = courant_ref[...]
    ahead = jnp.maximum(courant, 0.0)
    behind = jnp.minimum(courant, 0.0)
    return (centre - ahead * (centre - left) - behind * (right - centre)).astype(jnp.bfloat16)


def moments_kernel(dist_ref, basis_ref, out_ref):
    @pl.when(pl.program_id(0) == 0)
    def _():
        out_ref[...] = jnp.zeros_like(out_ref)

    out_ref[...] += jnp.dot(basis_ref[0], dist_ref[...], preferred_element_type=jnp.float32)


def relax_kernel(
    dist_ref, left_ref, right_ref, courant_ref, recon3_ref, gain_ref, keep_ref, out_ref,
):
    read = transport_block(dist_ref, left_ref, right_ref, courant_ref).astype(jnp.float32)
    gained = jnp.dot(recon3_ref[...], gain_ref[...], preferred_element_type=jnp.float32)
    out_ref[...] = (read * keep_ref[...] + gained).astype(out_ref.dtype)


def row_spec(width):
    return pl.BlockSpec((ROW_BLOCK, width), lambda i: (i, 0))


def full_spec(shape):
    return pl.BlockSpec(shape, lambda i: (0,) * len(shape))


def moments_call(dist, basis):
    rows, cells = dist.shape
    steps = rows // ROW_BLOCK
    height = basis.shape[0]
    blocks = basis.reshape(height, steps, ROW_BLOCK).transpose(1, 0, 2)
    return pl.pallas_call(
        moments_kernel,
        grid=(steps,),
        in_specs=[
            row_spec(cells),
            pl.BlockSpec((1, height, ROW_BLOCK), lambda i: (i, 0, 0)),
        ],
        out_specs=full_spec((height, cells)),
        out_shape=jax.ShapeDtypeStruct((height, cells), jnp.float32),
        compiler_params=pltpu.CompilerParams(dimension_semantics=("arbitrary",)),
        cost_estimate=pl.CostEstimate(
            flops=2 * rows * cells * height,
            bytes_accessed=rows * cells * 2 + height * cells * 4,
            transcendentals=0,
        ),
    )(dist, blocks)


def stencil_moments(dist, left, right, courant, basis):
    ahead = jnp.maximum(courant[:, 0], 0.0)
    behind = jnp.minimum(courant[:, 0], 0.0)
    weights = basis.astype(jnp.float32)
    stencil = [weights * (1.0 - ahead + behind)[None, :], weights * ahead[None, :], -weights * behind[None, :]]
    stacked = split_three(jnp.concatenate(stencil, axis=0))
    products = moments_call(dist, stacked)
    parts = products.reshape(3, 3, MOMENTS, dist.shape[1])
    parts = (parts[0] + parts[1]) + parts[2]
    edge_left = jnp.sum(stencil[1] * left[:, 0].astype(jnp.float32)[None, :], axis=1)
    edge_right = jnp.sum(stencil[2] * right[:, 0].astype(jnp.float32)[None, :], axis=1)
    from_left = jnp.concatenate([edge_left[:, None], parts[1][:, :-1]], axis=1)
    from_right = jnp.concatenate([parts[2][:, 1:], edge_right[:, None]], axis=1)
    return (parts[0] + from_left) + from_right


def relax_call(dist, left, right, courant, recon3, gain, keep):
    rows, cells = dist.shape
    steps = rows // ROW_BLOCK
    return pl.pallas_call(
        relax_kernel,
        grid=(steps,),
        in_specs=[
            row_spec(cells),
            row_spec(1),
            row_spec(1),
            row_spec(1),
            row_spec(recon3.shape[1]),
            full_spec(gain.shape),
            full_spec(keep.shape),
        ],
        out_specs=row_spec(cells),
        out_shape=jax.ShapeDtypeStruct((rows, cells), jnp.bfloat16),
        compiler_params=pltpu.CompilerParams(dimension_semantics=("parallel",)),
        cost_estimate=pl.CostEstimate(
            flops=2 * rows * cells * 60 + 10 * rows * cells,
            bytes_accessed=rows * cells * 4,
            transcendentals=0,
        ),
    )(dist, left, right, courant, recon3, gain, keep)


def split_three(values):
    first = lax.reduce_precision(values, exponent_bits=8, mantissa_bits=7)
    rest = values - first
    second = lax.reduce_precision(rest, exponent_bits=8, mantissa_bits=7)
    third = rest - second
    parts = [first, second, third]
    return jnp.concatenate([part.astype(jnp.bfloat16) for part in parts], axis=0)


def sect_sum(values):
    count = lax.axis_size("sect")
    total = values
    step = 1
    while step < count:
        pairs = [(i, i ^ step) for i in range(count)]
        total = total + lax.ppermute(total, "sect", pairs)
        step *= 2
    return total


def interface_rows(plenum_moments, iface_cell, width, base):
    count = lax.axis_size("sect")
    share = plenum_moments.shape[0] // count
    start = lax.axis_index("sect") * share
    coded = jnp.concatenate(
        [
            plenum_moments.astype(jnp.bfloat16),
            (iface_cell // 256).astype(jnp.bfloat16)[:, None],
            (iface_cell % 256).astype(jnp.bfloat16)[:, None],
        ],
        axis=1,
    )
    coded = lax.dynamic_slice_in_dim(coded, start, share, axis=0)
    peers = lax.axis_size("space")
    spread_out = jnp.broadcast_to(coded[None], (peers,) + coded.shape).reshape(peers * share, -1)
    gathered = lax.all_to_all(spread_out, "space", 0, 0, tiled=True)
    return fold_interface(gathered, width, base)


def fold_interface(gathered, width, base):
    low = width // CELL_HI
    rows = gathered[:, :MOMENTS]
    cells = gathered[:, MOMENTS].astype(jnp.int32) * 256 + gathered[:, MOMENTS + 1].astype(jnp.int32)
    local = cells - base
    valid = (local >= 0) & (local < width)
    upper = jnp.where(valid, local // low, -1)
    lower = local % low
    extended = jnp.concatenate([rows, jnp.ones((rows.shape[0], 1), jnp.bfloat16)], axis=1)
    pick_hi = (upper[:, None] == jnp.arange(CELL_HI, dtype=jnp.int32)[None, :]).astype(jnp.bfloat16)
    spread = (pick_hi[:, :, None] * extended[:, None, :]).reshape(rows.shape[0], -1)
    pick_lo = (lower[:, None] == jnp.arange(low, dtype=jnp.int32)[None, :]).astype(jnp.bfloat16)
    folded = lax.dot_general(
        spread, pick_lo, (((0,), (0,)), ((), ())), preferred_element_type=jnp.float32
    )
    return folded.reshape(CELL_HI, MOMENTS + 1, low).transpose(1, 0, 2).reshape(MOMENTS + 1, width)


def inject(closure, folded):
    fluid = folded[:MOMENTS]
    hit = folded[MOMENTS]
    return closure + hit[None, :] * (fluid - closure)


def ghost_walls(targets, ghost_source, ghost_owner, wall_cell):
    cells = targets.shape[1]
    peers = lax.axis_size("space")
    capacity = wall_cell.shape[2]
    slots = peers * capacity
    owner = ghost_owner[:, 0]
    marks = (owner[:, None] == jnp.arange(peers, dtype=jnp.int32)[None, :]).astype(jnp.int32)
    before = jnp.cumsum(marks, axis=0) - marks
    slot = jnp.sum(marks * before, axis=1)
    places = owner * capacity + slot
    at_place = (places[:, None] == jnp.arange(slots, dtype=jnp.int32)[None, :]).astype(jnp.int32)
    source_of = jnp.sum(at_place * (ghost_source[:, None] + 1), axis=0) - 1
    select = (jnp.arange(cells, dtype=jnp.int32)[:, None] == source_of[None, :]).astype(jnp.bfloat16)
    outgoing = jnp.dot(targets, select, preferred_element_type=jnp.float32).astype(jnp.bfloat16)
    arrived = lax.all_to_all(outgoing, "space", split_axis=1, concat_axis=1, tiled=True)
    walls = wall_cell.reshape(slots)
    land = (walls[:, None] == jnp.arange(cells, dtype=jnp.int32)[None, :]).astype(jnp.bfloat16)
    return jnp.dot(arrived, land, preferred_element_type=jnp.float32)


def per_device(
    dist,
    velocity,
    quad_weight,
    collision_rate,
    ghost_source,
    ghost_owner,
    wall_cell,
    plenum_moments,
    iface_cell,
):
    cells = dist.shape[1]
    courant = (COURANT_SCALE * velocity[0])[:, None]
    left, right = halo_columns(dist)
    partial_moments = stencil_moments(
        dist, left, right, courant, moment_basis(velocity, quad_weight)
    )
    slab_base = lax.axis_index("space") * cells
    moments = sect_sum(partial_moments)
    partial_rows = interface_rows(plenum_moments, iface_cell, cells, slab_base)
    rows = sect_sum(partial_rows.astype(jnp.bfloat16)).astype(jnp.float32)
    targets = inject(es_targets(moments), rows).astype(jnp.bfloat16)
    wall_moments = ghost_walls(targets, ghost_source, ghost_owner, wall_cell)
    recon = recon_basis(velocity)
    recon3 = jnp.concatenate([recon, recon, recon], axis=1)
    rate = collision_rate[None, :]
    gain = split_three(rate * targets.astype(jnp.float32) + WALL_SHARE * wall_moments)
    return relax_call(dist, left, right, courant, recon3, gain, 1.0 - rate)


def solution(mesh):
    in_specs = (
        P("sect", "space"),
        P(None, "sect"),
        P("sect"),
        P("space"),
        P("space"),
        P("space", None),
        P("space", None, None),
        P("space", None),
        P("space"),
    )
    out_specs = P("sect", "space")

    return jax.shard_map(per_device, mesh=mesh, in_specs=in_specs, out_specs=out_specs, check_vma=False)
```

```python
import jax
import jax.numpy as jnp
from jax import lax
from jax.experimental import pallas as pl
from jax.experimental.pallas import tpu as pltpu
from jax.sharding import PartitionSpec as P


NV = 8000
MOMENTS = 20


COURANT_SCALE = 0.6
ES_SHIFT = -0.5
WALL_SHARE = 0.5
ORDER_TWO = ((0, 0), (1, 1), (2, 2), (0, 1), (0, 2), (1, 2))
ORDER_THREE = (
    (0, 0, 0),
    (1, 1, 1),
    (2, 2, 2),
    (0, 0, 1),
    (0, 0, 2),
    (1, 1, 0),
    (1, 1, 2),
    (2, 2, 0),
    (2, 2, 1),
    (0, 1, 2),
)
RECON_NORMS = (
    1.0,
    1.0,
    1.0,
    1.0,
    2.0,
    2.0,
    2.0,
    1.0,
    1.0,
    1.0,
    6.0,
    6.0,
    6.0,
    2.0,
    2.0,
    2.0,
    2.0,
    2.0,
    2.0,
    1.0,
)
ROW_BLOCK = 400
CELL_HI = 8


def halo_columns(shard):
    count = lax.axis_size("space")
    length = shard.shape[1]
    up = [(i, i + 1) for i in range(count - 1)]
    down = [(j, i) for i, j in up]
    before = lax.ppermute(shard[:, length - 1 :], "space", up)
    after = lax.ppermute(shard[:, :1], "space", down)
    return before, after


def hermite_tables():
    factors = [[0, 0, 0]]
    corrections = [[4, 4, 4]]
    for i in range(3):
        factors.append([i + 1, 0, 0])
        corrections.append([4, 4, 4])
    for i, j in ORDER_TWO:
        factors.append([i + 1, j + 1, 0])
        corrections.append([0 if i == j else 4, 4, 4])
    for i, j, k in ORDER_THREE:
        factors.append([i + 1, j + 1, k + 1])
        corrections.append(
            [k + 1 if i == j else 4, j + 1 if i == k else 4, i + 1 if j == k else 4]
        )
    return factors, corrections


def hermite(velocity):
    factors, corrections = hermite_tables()
    width = velocity.shape[1]
    extended = jnp.concatenate(
        [jnp.ones((1, width), jnp.float32), velocity, jnp.zeros((1, width), jnp.float32)], axis=0
    )
    rows = jnp.arange(5, dtype=jnp.int32)

    def pick(column):
        chosen = jnp.array(column, dtype=jnp.int32)
        select = (chosen[:, None] == rows[None, :]).astype(jnp.float32)
        return jnp.sum(select[:, :, None] * extended[None, :, :], axis=1)

    first, second, third = [pick([f[n] for f in factors]) for n in range(3)]
    element = first * second * third
    for n in range(3):
        element = element - pick([c[n] for c in corrections])
    return element


def moment_basis(velocity, weight):
    return (hermite(velocity) * (weight / NV)[None, :]).astype(jnp.bfloat16)


def recon_basis(velocity):
    norms = jnp.array(RECON_NORMS, dtype=jnp.float32)
    return (hermite(velocity) / norms[:, None]).T.astype(jnp.bfloat16)


def es_targets(moments):
    density = moments[0]
    moving = [moments[1], moments[2], moments[3]]
    trace_sum = moments[4] + moments[5] + moments[6]
    second = [[None, None, None], [None, None, None], [None, None, None]]
    for n, (i, j) in enumerate(ORDER_TWO):
        element = (1.0 - ES_SHIFT) * moments[4 + n]
        if i == j:
            element = element + ES_SHIFT * trace_sum / 3.0
        second[i][j] = element
        second[j][i] = element
    stacked = [density] + moving + [second[i][j] for i, j in ORDER_TWO]
    for n, (i, j, k) in enumerate(ORDER_THREE):
        stacked.append(
            0.5 * moments[10 + n]
            + (moving[i] * second[j][k] + moving[j] * second[i][k] + moving[k] * second[i][j])
            / density
        )
    return jnp.stack(stacked)


def transport_block(dist_ref, left_ref, right_ref, courant_ref):
    centre = dist_ref[...].astype(jnp.float32)
    width = centre.shape[1]
    column = lax.broadcasted_iota(jnp.int32, (1, width), 1)
    left = jnp.where(
        column == 0, left_ref[...].astype(jnp.float32), pltpu.roll(centre, 1, 1)
    )
    right = jnp.where(
        column == width - 1,
        right_ref[...].astype(jnp.float32),
        pltpu.roll(centre, width - 1, 1),
    )
    courant = courant_ref[...]
    ahead = jnp.maximum(courant, 0.0)
    behind = jnp.minimum(courant, 0.0)
    return (centre - ahead * (centre - left) - behind * (right - centre)).astype(jnp.bfloat16)


def moments_kernel(dist_ref, basis_ref, out_ref):
    @pl.when(pl.program_id(0) == 0)
    def _():
        out_ref[...] = jnp.zeros_like(out_ref)

    out_ref[...] += jnp.dot(basis_ref[0], dist_ref[...], preferred_element_type=jnp.float32)


def relax_kernel(
    dist_ref, left_ref, right_ref, courant_ref, recon3_ref, gain_ref, keep_ref, out_ref,
):
    read = transport_block(dist_ref, left_ref, right_ref, courant_ref).astype(jnp.float32)
    gained = jnp.dot(recon3_ref[...], gain_ref[...], preferred_element_type=jnp.float32)
    out_ref[...] = (read * keep_ref[...] + gained).astype(out_ref.dtype)


def row_spec(width):
    return pl.BlockSpec((ROW_BLOCK, width), lambda i: (i, 0))


def full_spec(shape):
    return pl.BlockSpec(shape, lambda i: (0,) * len(shape))


def moments_call(dist, basis):
    rows, cells = dist.shape
    steps = rows // ROW_BLOCK
    height = basis.shape[0]
    blocks = basis.reshape(height, steps, ROW_BLOCK).transpose(1, 0, 2)
    return pl.pallas_call(
        moments_kernel,
        grid=(steps,),
        in_specs=[
            row_spec(cells),
            pl.BlockSpec((1, height, ROW_BLOCK), lambda i: (i, 0, 0)),
        ],
        out_specs=full_spec((height, cells)),
        out_shape=jax.ShapeDtypeStruct((height, cells), jnp.float32),
        compiler_params=pltpu.CompilerParams(dimension_semantics=("arbitrary",)),
        cost_estimate=pl.CostEstimate(
            flops=2 * rows * cells * height,
            bytes_accessed=rows * cells * 2 + height * cells * 4,
            transcendentals=0,
        ),
    )(dist, blocks)


def stencil_moments(dist, left, right, courant, basis):
    ahead = jnp.maximum(courant[:, 0], 0.0)
    behind = jnp.minimum(courant[:, 0], 0.0)
    weights = basis.astype(jnp.float32)
    stencil = [weights * (1.0 - ahead + behind)[None, :], weights * ahead[None, :], -weights * behind[None, :]]
    stacked = split_three(jnp.concatenate(stencil, axis=0))
    products = moments_call(dist, stacked)
    parts = products.reshape(3, 3, MOMENTS, dist.shape[1])
    parts = (parts[0] + parts[1]) + parts[2]
    edge_left = jnp.sum(stencil[1] * left[:, 0].astype(jnp.float32)[None, :], axis=1)
    edge_right = jnp.sum(stencil[2] * right[:, 0].astype(jnp.float32)[None, :], axis=1)
    from_left = jnp.concatenate([edge_left[:, None], parts[1][:, :-1]], axis=1)
    from_right = jnp.concatenate([parts[2][:, 1:], edge_right[:, None]], axis=1)
    return (parts[0] + from_left) + from_right


def relax_call(dist, left, right, courant, recon3, gain, keep):
    rows, cells = dist.shape
    steps = rows // ROW_BLOCK
    return pl.pallas_call(
        relax_kernel,
        grid=(steps,),
        in_specs=[
            row_spec(cells),
            row_spec(1),
            row_spec(1),
            row_spec(1),
            row_spec(recon3.shape[1]),
            full_spec(gain.shape),
            full_spec(keep.shape),
        ],
        out_specs=row_spec(cells),
        out_shape=jax.ShapeDtypeStruct((rows, cells), jnp.bfloat16),
        compiler_params=pltpu.CompilerParams(dimension_semantics=("parallel",)),
        cost_estimate=pl.CostEstimate(
            flops=2 * rows * cells * 60 + 10 * rows * cells,
            bytes_accessed=rows * cells * 4,
            transcendentals=0,
        ),
    )(dist, left, right, courant, recon3, gain, keep)


def split_three(values):
    first = lax.reduce_precision(values, exponent_bits=8, mantissa_bits=7)
    rest = values - first
    second = lax.reduce_precision(rest, exponent_bits=8, mantissa_bits=7)
    third = rest - second
    parts = [first, second, third]
    return jnp.concatenate([part.astype(jnp.bfloat16) for part in parts], axis=0)


def sect_sum(values):
    count = lax.axis_size("sect")
    total = values
    step = 1
    while step < count:
        pairs = [(i, i ^ step) for i in range(count)]
        total = total + lax.ppermute(total, "sect", pairs)
        step *= 2
    return total


def interface_rows(plenum_moments, iface_cell, width, base):
    count = lax.axis_size("sect")
    share = plenum_moments.shape[0] // count
    start = lax.axis_index("sect") * share
    coded = jnp.concatenate(
        [
            plenum_moments.astype(jnp.bfloat16),
            (iface_cell // 256).astype(jnp.bfloat16)[:, None],
            (iface_cell % 256).astype(jnp.bfloat16)[:, None],
        ],
        axis=1,
    )
    coded = lax.dynamic_slice_in_dim(coded, start, share, axis=0)
    peers = lax.axis_size("space")
    spread_out = jnp.broadcast_to(coded[None], (peers,) + coded.shape).reshape(peers * share, -1)
    gathered = lax.all_to_all(spread_out, "space", 0, 0, tiled=True)
    return fold_interface(gathered, width, base)


def fold_interface(gathered, width, base):
    low = width // CELL_HI
    rows = gathered[:, :MOMENTS]
    cells = gathered[:, MOMENTS].astype(jnp.int32) * 256 + gathered[:, MOMENTS + 1].astype(jnp.int32)
    local = cells - base
    valid = (local >= 0) & (local < width)
    upper = jnp.where(valid, local // low, -1)
    lower = local % low
    extended = jnp.concatenate([rows, jnp.ones((rows.shape[0], 1), jnp.bfloat16)], axis=1)
    pick_hi = (upper[:, None] == jnp.arange(CELL_HI, dtype=jnp.int32)[None, :]).astype(jnp.bfloat16)
    spread = (pick_hi[:, :, None] * extended[:, None, :]).reshape(rows.shape[0], -1)
    pick_lo = (lower[:, None] == jnp.arange(low, dtype=jnp.int32)[None, :]).astype(jnp.bfloat16)
    folded = lax.dot_general(
        spread, pick_lo, (((0,), (0,)), ((), ())), preferred_element_type=jnp.float32
    )
    return folded.reshape(CELL_HI, MOMENTS + 1, low).transpose(1, 0, 2).reshape(MOMENTS + 1, width)


def inject(closure, folded):
    fluid = folded[:MOMENTS]
    hit = folded[MOMENTS]
    return closure + hit[None, :] * (fluid - closure)


def ghost_tables(cells, ghost_source, ghost_owner, wall_cell):
    peers = lax.axis_size("space")
    capacity = wall_cell.shape[2]
    slots = peers * capacity
    owner = ghost_owner[:, 0]
    marks = (owner[:, None] == jnp.arange(peers, dtype=jnp.int32)[None, :]).astype(jnp.int32)
    before = jnp.cumsum(marks, axis=0) - marks
    slot = jnp.sum(marks * before, axis=1)
    places = owner * capacity + slot
    at_place = (places[:, None] == jnp.arange(slots, dtype=jnp.int32)[None, :]).astype(jnp.int32)
    source_of = jnp.sum(at_place * (ghost_source[:, None] + 1), axis=0) - 1
    select = (jnp.arange(cells, dtype=jnp.int32)[:, None] == source_of[None, :]).astype(jnp.bfloat16)
    walls = wall_cell.reshape(slots)
    land = (walls[:, None] == jnp.arange(cells, dtype=jnp.int32)[None, :]).astype(jnp.bfloat16)
    return select, land


def ghost_walls(targets, select, land):
    outgoing = jnp.dot(targets, select, preferred_element_type=jnp.float32).astype(jnp.bfloat16)
    arrived = lax.all_to_all(outgoing, "space", split_axis=1, concat_axis=1, tiled=True)
    return jnp.dot(arrived, land, preferred_element_type=jnp.float32)


def per_device(
    dist,
    velocity,
    quad_weight,
    collision_rate,
    ghost_source,
    ghost_owner,
    wall_cell,
    plenum_moments,
    iface_cell,
):
    cells = dist.shape[1]
    courant = (COURANT_SCALE * velocity[0])[:, None]
    left, right = halo_columns(dist)
    partial_moments = stencil_moments(
        dist, left, right, courant, moment_basis(velocity, quad_weight)
    )
    slab_base = lax.axis_index("space") * cells
    select, land = ghost_tables(cells, ghost_source, ghost_owner, wall_cell)
    select, land = lax.optimization_barrier((select, land))
    recon = recon_basis(velocity)
    recon3 = lax.optimization_barrier(jnp.concatenate([recon, recon, recon], axis=1))
    moments = sect_sum(partial_moments)
    partial_rows = interface_rows(plenum_moments, iface_cell, cells, slab_base)
    rows = sect_sum(partial_rows.astype(jnp.bfloat16)).astype(jnp.float32)
    targets = inject(es_targets(moments), rows).astype(jnp.bfloat16)
    wall_moments = ghost_walls(targets, select, land)
    rate = collision_rate[None, :]
    gain = split_three(rate * targets.astype(jnp.float32) + WALL_SHARE * wall_moments)
    return relax_call(dist, left, right, courant, recon3, gain, 1.0 - rate)


def solution(mesh):
    in_specs = (
        P("sect", "space"),
        P(None, "sect"),
        P("sect"),
        P("space"),
        P("space"),
        P("space", None),
        P("space", None, None),
        P("space", None),
        P("space"),
    )
    out_specs = P("sect", "space")

    return jax.shard_map(per_device, mesh=mesh, in_specs=in_specs, out_specs=out_specs, check_vma=False)
```

```python
import jax
import jax.numpy as jnp
from jax import lax
from jax.experimental import pallas as pl
from jax.experimental.pallas import tpu as pltpu
from jax.sharding import PartitionSpec as P


NV = 8000
MOMENTS = 20


COURANT_SCALE = 0.6
ES_SHIFT = -0.5
WALL_SHARE = 0.5
ORDER_TWO = ((0, 0), (1, 1), (2, 2), (0, 1), (0, 2), (1, 2))
ORDER_THREE = (
    (0, 0, 0),
    (1, 1, 1),
    (2, 2, 2),
    (0, 0, 1),
    (0, 0, 2),
    (1, 1, 0),
    (1, 1, 2),
    (2, 2, 0),
    (2, 2, 1),
    (0, 1, 2),
)
RECON_NORMS = (
    1.0,
    1.0,
    1.0,
    1.0,
    2.0,
    2.0,
    2.0,
    1.0,
    1.0,
    1.0,
    6.0,
    6.0,
    6.0,
    2.0,
    2.0,
    2.0,
    2.0,
    2.0,
    2.0,
    1.0,
)
ROW_BLOCK = 400
CHUNK = 16
CELL_HI = 8


def halo_columns(shard):
    count = lax.axis_size("space")
    length = shard.shape[1]
    up = [(i, i + 1) for i in range(count - 1)]
    down = [(j, i) for i, j in up]
    before = lax.ppermute(shard[:, length - 1 :], "space", up)
    after = lax.ppermute(shard[:, :1], "space", down)
    return before, after


def hermite_tables():
    factors = [[0, 0, 0]]
    corrections = [[4, 4, 4]]
    for i in range(3):
        factors.append([i + 1, 0, 0])
        corrections.append([4, 4, 4])
    for i, j in ORDER_TWO:
        factors.append([i + 1, j + 1, 0])
        corrections.append([0 if i == j else 4, 4, 4])
    for i, j, k in ORDER_THREE:
        factors.append([i + 1, j + 1, k + 1])
        corrections.append(
            [k + 1 if i == j else 4, j + 1 if i == k else 4, i + 1 if j == k else 4]
        )
    return factors, corrections


def hermite(velocity):
    factors, corrections = hermite_tables()
    width = velocity.shape[1]
    extended = jnp.concatenate(
        [jnp.ones((1, width), jnp.float32), velocity, jnp.zeros((1, width), jnp.float32)], axis=0
    )
    rows = jnp.arange(5, dtype=jnp.int32)

    def pick(column):
        chosen = jnp.array(column, dtype=jnp.int32)
        select = (chosen[:, None] == rows[None, :]).astype(jnp.float32)
        return jnp.sum(select[:, :, None] * extended[None, :, :], axis=1)

    first, second, third = [pick([f[n] for f in factors]) for n in range(3)]
    element = first * second * third
    for n in range(3):
        element = element - pick([c[n] for c in corrections])
    return element


def moment_basis(velocity, weight):
    return (hermite(velocity) * (weight / NV)[None, :]).astype(jnp.bfloat16)


def recon_basis(velocity):
    norms = jnp.array(RECON_NORMS, dtype=jnp.float32)
    return (hermite(velocity) / norms[:, None]).T.astype(jnp.bfloat16)


def es_targets(moments):
    density = moments[0]
    moving = [moments[1], moments[2], moments[3]]
    trace_sum = moments[4] + moments[5] + moments[6]
    second = [[None, None, None], [None, None, None], [None, None, None]]
    for n, (i, j) in enumerate(ORDER_TWO):
        element = (1.0 - ES_SHIFT) * moments[4 + n]
        if i == j:
            element = element + ES_SHIFT * trace_sum / 3.0
        second[i][j] = element
        second[j][i] = element
    stacked = [density] + moving + [second[i][j] for i, j in ORDER_TWO]
    for n, (i, j, k) in enumerate(ORDER_THREE):
        stacked.append(
            0.5 * moments[10 + n]
            + (moving[i] * second[j][k] + moving[j] * second[i][k] + moving[k] * second[i][j])
            / density
        )
    return jnp.stack(stacked)


def transport_block(dist_ref, left_ref, right_ref, courant_ref):
    centre = dist_ref[...].astype(jnp.float32)
    width = centre.shape[1]
    column = lax.broadcasted_iota(jnp.int32, (1, width), 1)
    left = jnp.where(
        column == 0, left_ref[...].astype(jnp.float32), pltpu.roll(centre, 1, 1)
    )
    right = jnp.where(
        column == width - 1,
        right_ref[...].astype(jnp.float32),
        pltpu.roll(centre, width - 1, 1),
    )
    courant = courant_ref[...]
    ahead = jnp.maximum(courant, 0.0)
    behind = jnp.minimum(courant, 0.0)
    return (centre - ahead * (centre - left) - behind * (right - centre)).astype(jnp.bfloat16)


def moments_kernel(dist_ref, basis_ref, out_ref):
    @pl.when(pl.program_id(0) == 0)
    def _():
        out_ref[...] = jnp.zeros_like(out_ref)

    out_ref[...] += jnp.dot(basis_ref[0], dist_ref[...], preferred_element_type=jnp.float32)


def relax_kernel(
    dist_ref, left_ref, right_ref, courant_ref, recon3_ref, gain_ref, keep_ref, out_ref, gained_ref,
):
    gained_ref[...] = jnp.dot(recon3_ref[...], gain_ref[...], preferred_element_type=jnp.float32)
    keep = keep_ref[...]

    def chunk(step, carry):
        rows = pl.ds(pl.multiple_of(step * CHUNK, CHUNK), CHUNK)
        read = transport_block(
            dist_ref.at[rows], left_ref.at[rows], right_ref.at[rows], courant_ref.at[rows]
        ).astype(jnp.float32)
        out_ref[rows, :] = (read * keep + gained_ref[rows, :]).astype(out_ref.dtype)
        return carry

    lax.fori_loop(0, ROW_BLOCK // CHUNK, chunk, 0, unroll=True)


def row_spec(width):
    return pl.BlockSpec((ROW_BLOCK, width), lambda i: (i, 0))


def full_spec(shape):
    return pl.BlockSpec(shape, lambda i: (0,) * len(shape))


def moments_call(dist, basis):
    rows, cells = dist.shape
    steps = rows // ROW_BLOCK
    height = basis.shape[0]
    blocks = basis.reshape(height, steps, ROW_BLOCK).transpose(1, 0, 2)
    return pl.pallas_call(
        moments_kernel,
        grid=(steps,),
        in_specs=[
            row_spec(cells),
            pl.BlockSpec((1, height, ROW_BLOCK), lambda i: (i, 0, 0)),
        ],
        out_specs=full_spec((height, cells)),
        out_shape=jax.ShapeDtypeStruct((height, cells), jnp.float32),
        compiler_params=pltpu.CompilerParams(dimension_semantics=("arbitrary",)),
        cost_estimate=pl.CostEstimate(
            flops=2 * rows * cells * height,
            bytes_accessed=rows * cells * 2 + height * cells * 4,
            transcendentals=0,
        ),
    )(dist, blocks)


def stencil_moments(dist, left, right, courant, basis):
    ahead = jnp.maximum(courant[:, 0], 0.0)
    behind = jnp.minimum(courant[:, 0], 0.0)
    weights = basis.astype(jnp.float32)
    stencil = [weights * (1.0 - ahead + behind)[None, :], weights * ahead[None, :], -weights * behind[None, :]]
    stacked = split_three(jnp.concatenate(stencil, axis=0))
    products = moments_call(dist, stacked)
    parts = products.reshape(3, 3, MOMENTS, dist.shape[1])
    parts = (parts[0] + parts[1]) + parts[2]
    edge_left = jnp.sum(stencil[1] * left[:, 0].astype(jnp.float32)[None, :], axis=1)
    edge_right = jnp.sum(stencil[2] * right[:, 0].astype(jnp.float32)[None, :], axis=1)
    from_left = jnp.concatenate([edge_left[:, None], parts[1][:, :-1]], axis=1)
    from_right = jnp.concatenate([parts[2][:, 1:], edge_right[:, None]], axis=1)
    return (parts[0] + from_left) + from_right


def relax_call(dist, left, right, courant, recon3, gain, keep):
    rows, cells = dist.shape
    steps = rows // ROW_BLOCK
    return pl.pallas_call(
        relax_kernel,
        grid=(steps,),
        in_specs=[
            row_spec(cells),
            row_spec(1),
            row_spec(1),
            row_spec(1),
            row_spec(recon3.shape[1]),
            full_spec(gain.shape),
            full_spec(keep.shape),
        ],
        out_specs=row_spec(cells),
        out_shape=jax.ShapeDtypeStruct((rows, cells), jnp.bfloat16),
        scratch_shapes=[pltpu.VMEM((ROW_BLOCK, cells), jnp.float32)],
        compiler_params=pltpu.CompilerParams(dimension_semantics=("parallel",)),
        cost_estimate=pl.CostEstimate(
            flops=2 * rows * cells * 60 + 10 * rows * cells,
            bytes_accessed=rows * cells * 4,
            transcendentals=0,
        ),
    )(dist, left, right, courant, recon3, gain, keep)


def split_three(values):
    first = lax.reduce_precision(values, exponent_bits=8, mantissa_bits=7)
    rest = values - first
    second = lax.reduce_precision(rest, exponent_bits=8, mantissa_bits=7)
    third = rest - second
    parts = [first, second, third]
    return jnp.concatenate([part.astype(jnp.bfloat16) for part in parts], axis=0)


def sect_sum(values):
    count = lax.axis_size("sect")
    total = values
    step = 1
    while step < count:
        pairs = [(i, i ^ step) for i in range(count)]
        total = total + lax.ppermute(total, "sect", pairs)
        step *= 2
    return total


def interface_rows(plenum_moments, iface_cell, width, base):
    count = lax.axis_size("sect")
    share = plenum_moments.shape[0] // count
    start = lax.axis_index("sect") * share
    coded = jnp.concatenate(
        [
            plenum_moments.astype(jnp.bfloat16),
            (iface_cell // 256).astype(jnp.bfloat16)[:, None],
            (iface_cell % 256).astype(jnp.bfloat16)[:, None],
        ],
        axis=1,
    )
    coded = lax.dynamic_slice_in_dim(coded, start, share, axis=0)
    peers = lax.axis_size("space")
    spread_out = jnp.broadcast_to(coded[None], (peers,) + coded.shape).reshape(peers * share, -1)
    gathered = lax.all_to_all(spread_out, "space", 0, 0, tiled=True)
    return fold_interface(gathered, width, base)


def fold_interface(gathered, width, base):
    low = width // CELL_HI
    rows = gathered[:, :MOMENTS]
    cells = gathered[:, MOMENTS].astype(jnp.int32) * 256 + gathered[:, MOMENTS + 1].astype(jnp.int32)
    local = cells - base
    valid = (local >= 0) & (local < width)
    upper = jnp.where(valid, local // low, -1)
    lower = local % low
    extended = jnp.concatenate([rows, jnp.ones((rows.shape[0], 1), jnp.bfloat16)], axis=1)
    pick_hi = (upper[:, None] == jnp.arange(CELL_HI, dtype=jnp.int32)[None, :]).astype(jnp.bfloat16)
    spread = (pick_hi[:, :, None] * extended[:, None, :]).reshape(rows.shape[0], -1)
    pick_lo = (lower[:, None] == jnp.arange(low, dtype=jnp.int32)[None, :]).astype(jnp.bfloat16)
    folded = lax.dot_general(
        spread, pick_lo, (((0,), (0,)), ((), ())), preferred_element_type=jnp.float32
    )
    return folded.reshape(CELL_HI, MOMENTS + 1, low).transpose(1, 0, 2).reshape(MOMENTS + 1, width)


def inject(closure, folded):
    fluid = folded[:MOMENTS]
    hit = folded[MOMENTS]
    return closure + hit[None, :] * (fluid - closure)


def ghost_tables(cells, ghost_source, ghost_owner, wall_cell):
    peers = lax.axis_size("space")
    capacity = wall_cell.shape[2]
    slots = peers * capacity
    owner = ghost_owner[:, 0]
    marks = (owner[:, None] == jnp.arange(peers, dtype=jnp.int32)[None, :]).astype(jnp.int32)
    before = jnp.cumsum(marks, axis=0) - marks
    slot = jnp.sum(marks * before, axis=1)
    places = owner * capacity + slot
    at_place = (places[:, None] == jnp.arange(slots, dtype=jnp.int32)[None, :]).astype(jnp.int32)
    source_of = jnp.sum(at_place * (ghost_source[:, None] + 1), axis=0) - 1
    select = (jnp.arange(cells, dtype=jnp.int32)[:, None] == source_of[None, :]).astype(jnp.bfloat16)
    walls = wall_cell.reshape(slots)
    land = (walls[:, None] == jnp.arange(cells, dtype=jnp.int32)[None, :]).astype(jnp.bfloat16)
    return select, land


def ghost_walls(targets, select, land):
    outgoing = jnp.dot(targets, select, preferred_element_type=jnp.float32).astype(jnp.bfloat16)
    arrived = lax.all_to_all(outgoing, "space", split_axis=1, concat_axis=1, tiled=True)
    return jnp.dot(arrived, land, preferred_element_type=jnp.float32)


def per_device(
    dist,
    velocity,
    quad_weight,
    collision_rate,
    ghost_source,
    ghost_owner,
    wall_cell,
    plenum_moments,
    iface_cell,
):
    cells = dist.shape[1]
    courant = (COURANT_SCALE * velocity[0])[:, None]
    left, right = halo_columns(dist)
    partial_moments = stencil_moments(
        dist, left, right, courant, moment_basis(velocity, quad_weight)
    )
    slab_base = lax.axis_index("space") * cells
    select, land = ghost_tables(cells, ghost_source, ghost_owner, wall_cell)
    select, land = lax.optimization_barrier((select, land))
    recon = recon_basis(velocity)
    recon3 = lax.optimization_barrier(jnp.concatenate([recon, recon, recon], axis=1))
    moments = sect_sum(partial_moments)
    partial_rows = interface_rows(plenum_moments, iface_cell, cells, slab_base)
    rows = sect_sum(partial_rows.astype(jnp.bfloat16)).astype(jnp.float32)
    targets = inject(es_targets(moments), rows).astype(jnp.bfloat16)
    wall_moments = ghost_walls(targets, select, land)
    rate = collision_rate[None, :]
    gain = split_three(rate * targets.astype(jnp.float32) + WALL_SHARE * wall_moments)
    return relax_call(dist, left, right, courant, recon3, gain, 1.0 - rate)


def solution(mesh):
    in_specs = (
        P("sect", "space"),
        P(None, "sect"),
        P("sect"),
        P("space"),
        P("space"),
        P("space", None),
        P("space", None, None),
        P("space", None),
        P("space"),
    )
    out_specs = P("sect", "space")

    return jax.shard_map(per_device, mesh=mesh, in_specs=in_specs, out_specs=out_specs, check_vma=False)
```

```python
import jax
import jax.numpy as jnp
from jax import lax
from jax.experimental import pallas as pl
from jax.experimental.pallas import tpu as pltpu
from jax.sharding import PartitionSpec as P


NV = 8000
MOMENTS = 20


COURANT_SCALE = 0.6
ES_SHIFT = -0.5
WALL_SHARE = 0.5
ORDER_TWO = ((0, 0), (1, 1), (2, 2), (0, 1), (0, 2), (1, 2))
ORDER_THREE = (
    (0, 0, 0),
    (1, 1, 1),
    (2, 2, 2),
    (0, 0, 1),
    (0, 0, 2),
    (1, 1, 0),
    (1, 1, 2),
    (2, 2, 0),
    (2, 2, 1),
    (0, 1, 2),
)
RECON_NORMS = (
    1.0,
    1.0,
    1.0,
    1.0,
    2.0,
    2.0,
    2.0,
    1.0,
    1.0,
    1.0,
    6.0,
    6.0,
    6.0,
    2.0,
    2.0,
    2.0,
    2.0,
    2.0,
    2.0,
    1.0,
)
ROW_BLOCK = 400
CHUNK = 16
CELL_HI = 8


def halo_columns(shard):
    count = lax.axis_size("space")
    length = shard.shape[1]
    up = [(i, i + 1) for i in range(count - 1)]
    down = [(j, i) for i, j in up]
    before = lax.ppermute(shard[:, length - 1 :], "space", up)
    after = lax.ppermute(shard[:, :1], "space", down)
    return before, after


def hermite_tables():
    factors = [[0, 0, 0]]
    corrections = [[4, 4, 4]]
    for i in range(3):
        factors.append([i + 1, 0, 0])
        corrections.append([4, 4, 4])
    for i, j in ORDER_TWO:
        factors.append([i + 1, j + 1, 0])
        corrections.append([0 if i == j else 4, 4, 4])
    for i, j, k in ORDER_THREE:
        factors.append([i + 1, j + 1, k + 1])
        corrections.append(
            [k + 1 if i == j else 4, j + 1 if i == k else 4, i + 1 if j == k else 4]
        )
    return factors, corrections


def hermite(velocity):
    factors, corrections = hermite_tables()
    width = velocity.shape[1]
    extended = jnp.concatenate(
        [jnp.ones((1, width), jnp.float32), velocity, jnp.zeros((1, width), jnp.float32)], axis=0
    )
    rows = jnp.arange(5, dtype=jnp.int32)

    def pick(column):
        chosen = jnp.array(column, dtype=jnp.int32)
        select = (chosen[:, None] == rows[None, :]).astype(jnp.float32)
        return jnp.sum(select[:, :, None] * extended[None, :, :], axis=1)

    first, second, third = [pick([f[n] for f in factors]) for n in range(3)]
    element = first * second * third
    for n in range(3):
        element = element - pick([c[n] for c in corrections])
    return element


def moment_basis(velocity, weight):
    return (hermite(velocity) * (weight / NV)[None, :]).astype(jnp.bfloat16)


def recon_basis(velocity):
    norms = jnp.array(RECON_NORMS, dtype=jnp.float32)
    return (hermite(velocity) / norms[:, None]).T.astype(jnp.bfloat16)


def es_targets(moments):
    density = moments[0]
    moving = [moments[1], moments[2], moments[3]]
    trace_sum = moments[4] + moments[5] + moments[6]
    second = [[None, None, None], [None, None, None], [None, None, None]]
    for n, (i, j) in enumerate(ORDER_TWO):
        element = (1.0 - ES_SHIFT) * moments[4 + n]
        if i == j:
            element = element + ES_SHIFT * trace_sum / 3.0
        second[i][j] = element
        second[j][i] = element
    stacked = [density] + moving + [second[i][j] for i, j in ORDER_TWO]
    for n, (i, j, k) in enumerate(ORDER_THREE):
        stacked.append(
            0.5 * moments[10 + n]
            + (moving[i] * second[j][k] + moving[j] * second[i][k] + moving[k] * second[i][j])
            / density
        )
    return jnp.stack(stacked)


def transport_block(dist_ref, left_ref, right_ref, courant_ref):
    centre = dist_ref[...].astype(jnp.float32)
    width = centre.shape[1]
    column = lax.broadcasted_iota(jnp.int32, (1, width), 1)
    left = jnp.where(
        column == 0, left_ref[...].astype(jnp.float32), pltpu.roll(centre, 1, 1)
    )
    right = jnp.where(
        column == width - 1,
        right_ref[...].astype(jnp.float32),
        pltpu.roll(centre, width - 1, 1),
    )
    courant = courant_ref[...]
    ahead = jnp.maximum(courant, 0.0)
    behind = jnp.minimum(courant, 0.0)
    return (centre - ahead * (centre - left) - behind * (right - centre)).astype(jnp.bfloat16)


def moments_kernel(dist_ref, basis_ref, out_ref):
    @pl.when(pl.program_id(0) == 0)
    def _():
        out_ref[...] = jnp.zeros_like(out_ref)

    out_ref[...] += jnp.dot(basis_ref[0], dist_ref[...], preferred_element_type=jnp.float32)


def relax_kernel(
    dist_ref, left_ref, right_ref, courant_ref, recon3_ref, gain_ref, keep_ref, out_ref, gained_ref,
):
    gained_ref[...] = jnp.dot(recon3_ref[...], gain_ref[...], preferred_element_type=jnp.float32)
    keep = keep_ref[...]

    def chunk(step, carry):
        rows = pl.ds(pl.multiple_of(step * CHUNK, CHUNK), CHUNK)
        read = transport_block(
            dist_ref.at[rows], left_ref.at[rows], right_ref.at[rows], courant_ref.at[rows]
        ).astype(jnp.float32)
        out_ref[rows, :] = (read * keep + gained_ref[rows, :]).astype(out_ref.dtype)
        return carry

    lax.fori_loop(0, ROW_BLOCK // CHUNK, chunk, 0, unroll=True)


def row_spec(width):
    return pl.BlockSpec((ROW_BLOCK, width), lambda i: (i, 0))


def full_spec(shape):
    return pl.BlockSpec(shape, lambda i: (0,) * len(shape))


def moments_call(dist, basis):
    rows, cells = dist.shape
    steps = rows // ROW_BLOCK
    height = basis.shape[0]
    blocks = basis.reshape(height, steps, ROW_BLOCK).transpose(1, 0, 2)
    return pl.pallas_call(
        moments_kernel,
        grid=(steps,),
        in_specs=[
            row_spec(cells),
            pl.BlockSpec((1, height, ROW_BLOCK), lambda i: (i, 0, 0)),
        ],
        out_specs=full_spec((height, cells)),
        out_shape=jax.ShapeDtypeStruct((height, cells), jnp.float32),
        compiler_params=pltpu.CompilerParams(dimension_semantics=("arbitrary",)),
        cost_estimate=pl.CostEstimate(
            flops=2 * rows * cells * height,
            bytes_accessed=rows * cells * 2 + height * cells * 4,
            transcendentals=0,
        ),
    )(dist, blocks)


def stencil_moments(dist, left, right, courant, basis):
    ahead = jnp.maximum(courant[:, 0], 0.0)
    behind = jnp.minimum(courant[:, 0], 0.0)
    weights = basis.astype(jnp.float32)
    stencil = [weights * (1.0 - ahead + behind)[None, :], weights * ahead[None, :], -weights * behind[None, :]]
    stacked = split_three(jnp.concatenate(stencil, axis=0))
    products = moments_call(dist, stacked)
    parts = products.reshape(3, 3, MOMENTS, dist.shape[1])
    parts = (parts[0] + parts[1]) + parts[2]
    edge_left = jnp.sum(stencil[1] * left[:, 0].astype(jnp.float32)[None, :], axis=1)
    edge_right = jnp.sum(stencil[2] * right[:, 0].astype(jnp.float32)[None, :], axis=1)
    from_left = jnp.concatenate([edge_left[:, None], parts[1][:, :-1]], axis=1)
    from_right = jnp.concatenate([parts[2][:, 1:], edge_right[:, None]], axis=1)
    return (parts[0] + from_left) + from_right


def relax_call(dist, left, right, courant, recon3, gain, keep):
    rows, cells = dist.shape
    steps = rows // ROW_BLOCK
    return pl.pallas_call(
        relax_kernel,
        grid=(steps,),
        in_specs=[
            row_spec(cells),
            row_spec(1),
            row_spec(1),
            row_spec(1),
            row_spec(recon3.shape[1]),
            full_spec(gain.shape),
            full_spec(keep.shape),
        ],
        out_specs=row_spec(cells),
        out_shape=jax.ShapeDtypeStruct((rows, cells), jnp.bfloat16),
        scratch_shapes=[pltpu.VMEM((ROW_BLOCK, cells), jnp.float32)],
        compiler_params=pltpu.CompilerParams(dimension_semantics=("parallel",)),
        cost_estimate=pl.CostEstimate(
            flops=2 * rows * cells * 60 + 10 * rows * cells,
            bytes_accessed=rows * cells * 4,
            transcendentals=0,
        ),
    )(dist, left, right, courant, recon3, gain, keep)


def split_three(values):
    first = lax.reduce_precision(values, exponent_bits=8, mantissa_bits=7)
    rest = values - first
    second = lax.reduce_precision(rest, exponent_bits=8, mantissa_bits=7)
    third = rest - second
    parts = [first, second, third]
    return jnp.concatenate([part.astype(jnp.bfloat16) for part in parts], axis=0)


def sect_sum(values):
    count = lax.axis_size("sect")
    total = values
    step = 1
    while step < count:
        pairs = [(i, i ^ step) for i in range(count)]
        total = total + lax.ppermute(total, "sect", pairs)
        step *= 2
    return total


def interface_rows(plenum_moments, iface_cell, width, base):
    count = lax.axis_size("sect")
    share = plenum_moments.shape[0] // count
    start = lax.axis_index("sect") * share
    coded = jnp.concatenate(
        [
            plenum_moments.astype(jnp.bfloat16),
            (iface_cell // 256).astype(jnp.bfloat16)[:, None],
            (iface_cell % 256).astype(jnp.bfloat16)[:, None],
        ],
        axis=1,
    )
    coded = lax.dynamic_slice_in_dim(coded, start, share, axis=0)
    peers = lax.axis_size("space")
    spread_out = jnp.broadcast_to(coded[None], (peers,) + coded.shape).reshape(peers * share, -1)
    gathered = lax.all_to_all(spread_out, "space", 0, 0, tiled=True)
    return fold_interface(gathered, width, base)


def fold_interface(gathered, width, base):
    low = width // CELL_HI
    rows = gathered[:, :MOMENTS]
    cells = gathered[:, MOMENTS].astype(jnp.int32) * 256 + gathered[:, MOMENTS + 1].astype(jnp.int32)
    local = cells - base
    valid = (local >= 0) & (local < width)
    upper = jnp.where(valid, local // low, -1)
    lower = local % low
    extended = jnp.concatenate([rows, jnp.ones((rows.shape[0], 1), jnp.bfloat16)], axis=1)
    pick_hi = (upper[:, None] == jnp.arange(CELL_HI, dtype=jnp.int32)[None, :]).astype(jnp.bfloat16)
    spread = (pick_hi[:, :, None] * extended[:, None, :]).reshape(rows.shape[0], -1)
    pick_lo = (lower[:, None] == jnp.arange(low, dtype=jnp.int32)[None, :]).astype(jnp.bfloat16)
    folded = lax.dot_general(
        spread, pick_lo, (((0,), (0,)), ((), ())), preferred_element_type=jnp.float32
    )
    return folded.reshape(CELL_HI, MOMENTS + 1, low).transpose(1, 0, 2).reshape(MOMENTS + 1, width)


def inject(closure, folded):
    fluid = folded[:MOMENTS]
    hit = folded[MOMENTS]
    return closure + hit[None, :] * (fluid - closure)


def ghost_tables(cells, ghost_source, ghost_owner, wall_cell):
    peers = lax.axis_size("space")
    capacity = wall_cell.shape[2]
    slots = peers * capacity
    owner = ghost_owner[:, 0]
    marks = (owner[:, None] == jnp.arange(peers, dtype=jnp.int32)[None, :]).astype(jnp.int32)
    before = jnp.cumsum(marks, axis=0) - marks
    slot = jnp.sum(marks * before, axis=1)
    places = owner * capacity + slot
    at_place = (places[:, None] == jnp.arange(slots, dtype=jnp.int32)[None, :]).astype(jnp.int32)
    source_of = jnp.sum(at_place * (ghost_source[:, None] + 1), axis=0) - 1
    select = (jnp.arange(cells, dtype=jnp.int32)[:, None] == source_of[None, :]).astype(jnp.bfloat16)
    walls = wall_cell.reshape(slots)
    land = (walls[:, None] == jnp.arange(cells, dtype=jnp.int32)[None, :]).astype(jnp.bfloat16)
    return select, land


def ghost_walls(targets, select, land):
    outgoing = jnp.dot(targets, select, preferred_element_type=jnp.float32).astype(jnp.bfloat16)
    arrived = lax.all_to_all(outgoing, "space", split_axis=1, concat_axis=1, tiled=True)
    return jnp.dot(arrived, land, preferred_element_type=jnp.float32)


def per_device(
    dist,
    velocity,
    quad_weight,
    collision_rate,
    ghost_source,
    ghost_owner,
    wall_cell,
    plenum_moments,
    iface_cell,
):
    cells = dist.shape[1]
    courant = (COURANT_SCALE * velocity[0])[:, None]
    left, right = halo_columns(dist)
    partial_moments = stencil_moments(
        dist, left, right, courant, moment_basis(velocity, quad_weight)
    )
    slab_base = lax.axis_index("space") * cells
    select, land = ghost_tables(cells, ghost_source, ghost_owner, wall_cell)
    select, land = lax.optimization_barrier((select, land))
    recon = recon_basis(velocity)
    recon3 = lax.optimization_barrier(jnp.concatenate([recon, recon, recon], axis=1))
    partial_rows = interface_rows(plenum_moments, iface_cell, cells, slab_base)
    summed = sect_sum(jnp.concatenate([partial_moments, partial_rows], axis=0))
    targets = inject(es_targets(summed[:MOMENTS]), summed[MOMENTS:]).astype(jnp.bfloat16)
    wall_moments = ghost_walls(targets, select, land)
    rate = collision_rate[None, :]
    gain = split_three(rate * targets.astype(jnp.float32) + WALL_SHARE * wall_moments)
    return relax_call(dist, left, right, courant, recon3, gain, 1.0 - rate)


def solution(mesh):
    in_specs = (
        P("sect", "space"),
        P(None, "sect"),
        P("sect"),
        P("space"),
        P("space"),
        P("space", None),
        P("space", None, None),
        P("space", None),
        P("space"),
    )
    out_specs = P("sect", "space")

    return jax.shard_map(per_device, mesh=mesh, in_specs=in_specs, out_specs=out_specs, check_vma=False)
```

```python
import jax
import jax.numpy as jnp
from jax import lax
from jax.experimental import pallas as pl
from jax.experimental.pallas import tpu as pltpu
from jax.sharding import PartitionSpec as P


NV = 8000
MOMENTS = 20


COURANT_SCALE = 0.6
ES_SHIFT = -0.5
WALL_SHARE = 0.5
ORDER_TWO = ((0, 0), (1, 1), (2, 2), (0, 1), (0, 2), (1, 2))
ORDER_THREE = (
    (0, 0, 0),
    (1, 1, 1),
    (2, 2, 2),
    (0, 0, 1),
    (0, 0, 2),
    (1, 1, 0),
    (1, 1, 2),
    (2, 2, 0),
    (2, 2, 1),
    (0, 1, 2),
)
RECON_NORMS = (
    1.0,
    1.0,
    1.0,
    1.0,
    2.0,
    2.0,
    2.0,
    1.0,
    1.0,
    1.0,
    6.0,
    6.0,
    6.0,
    2.0,
    2.0,
    2.0,
    2.0,
    2.0,
    2.0,
    1.0,
)
ROW_BLOCK = 400
CHUNK = 16
CELL_HI = 8


def halo_columns(shard):
    count = lax.axis_size("space")
    length = shard.shape[1]
    up = [(i, i + 1) for i in range(count - 1)]
    down = [(j, i) for i, j in up]
    before = lax.ppermute(shard[:, length - 1 :], "space", up)
    after = lax.ppermute(shard[:, :1], "space", down)
    return before, after


def hermite_tables():
    factors = [[0, 0, 0]]
    corrections = [[4, 4, 4]]
    for i in range(3):
        factors.append([i + 1, 0, 0])
        corrections.append([4, 4, 4])
    for i, j in ORDER_TWO:
        factors.append([i + 1, j + 1, 0])
        corrections.append([0 if i == j else 4, 4, 4])
    for i, j, k in ORDER_THREE:
        factors.append([i + 1, j + 1, k + 1])
        corrections.append(
            [k + 1 if i == j else 4, j + 1 if i == k else 4, i + 1 if j == k else 4]
        )
    return factors, corrections


def hermite(velocity):
    factors, corrections = hermite_tables()
    width = velocity.shape[1]
    extended = jnp.concatenate(
        [jnp.ones((1, width), jnp.float32), velocity, jnp.zeros((1, width), jnp.float32)], axis=0
    )

    def pick(column):
        chosen = jnp.array(column, dtype=jnp.int32)
        total = None
        for m in range(5):
            term = (chosen == m).astype(jnp.float32)[:, None] * extended[m][None, :]
            total = term if total is None else total + term
        return total

    first, second, third = [pick([f[n] for f in factors]) for n in range(3)]
    element = first * second * third
    for n in range(3):
        element = element - pick([c[n] for c in corrections])
    return element


def moment_basis(velocity, weight):
    return (hermite(velocity) * (weight / NV)[None, :]).astype(jnp.bfloat16)


def recon_basis(velocity):
    norms = jnp.array(RECON_NORMS, dtype=jnp.float32)
    return (hermite(velocity) / norms[:, None]).T.astype(jnp.bfloat16)


def es_targets(moments):
    density = moments[0]
    moving = [moments[1], moments[2], moments[3]]
    trace_sum = moments[4] + moments[5] + moments[6]
    second = [[None, None, None], [None, None, None], [None, None, None]]
    for n, (i, j) in enumerate(ORDER_TWO):
        element = (1.0 - ES_SHIFT) * moments[4 + n]
        if i == j:
            element = element + ES_SHIFT * trace_sum / 3.0
        second[i][j] = element
        second[j][i] = element
    stacked = [density] + moving + [second[i][j] for i, j in ORDER_TWO]
    for n, (i, j, k) in enumerate(ORDER_THREE):
        stacked.append(
            0.5 * moments[10 + n]
            + (moving[i] * second[j][k] + moving[j] * second[i][k] + moving[k] * second[i][j])
            / density
        )
    return jnp.stack(stacked)


def transport_block(dist_ref, left_ref, right_ref, courant_ref):
    centre = dist_ref[...].astype(jnp.float32)
    width = centre.shape[1]
    column = lax.broadcasted_iota(jnp.int32, (1, width), 1)
    left = jnp.where(
        column == 0, left_ref[...].astype(jnp.float32), pltpu.roll(centre, 1, 1)
    )
    right = jnp.where(
        column == width - 1,
        right_ref[...].astype(jnp.float32),
        pltpu.roll(centre, width - 1, 1),
    )
    courant = courant_ref[...]
    ahead = jnp.maximum(courant, 0.0)
    behind = jnp.minimum(courant, 0.0)
    return (centre - ahead * (centre - left) - behind * (right - centre)).astype(jnp.bfloat16)


def moments_kernel(dist_ref, basis_ref, out_ref):
    @pl.when(pl.program_id(0) == 0)
    def _():
        out_ref[...] = jnp.zeros_like(out_ref)

    out_ref[...] += jnp.dot(basis_ref[0], dist_ref[...], preferred_element_type=jnp.float32)


def relax_kernel(
    dist_ref, left_ref, right_ref, courant_ref, recon3_ref, gain_ref, keep_ref, out_ref, gained_ref,
):
    gained_ref[...] = jnp.dot(recon3_ref[...], gain_ref[...], preferred_element_type=jnp.float32)
    keep = keep_ref[...]

    def chunk(step, carry):
        rows = pl.ds(pl.multiple_of(step * CHUNK, CHUNK), CHUNK)
        read = transport_block(
            dist_ref.at[rows], left_ref.at[rows], right_ref.at[rows], courant_ref.at[rows]
        ).astype(jnp.float32)
        out_ref[rows, :] = (read * keep + gained_ref[rows, :]).astype(out_ref.dtype)
        return carry

    lax.fori_loop(0, ROW_BLOCK // CHUNK, chunk, 0, unroll=True)


def row_spec(width):
    return pl.BlockSpec((ROW_BLOCK, width), lambda i: (i, 0))


def full_spec(shape):
    return pl.BlockSpec(shape, lambda i: (0,) * len(shape))


def moments_call(dist, basis):
    rows, cells = dist.shape
    steps = rows // ROW_BLOCK
    height = basis.shape[0]
    blocks = basis.reshape(height, steps, ROW_BLOCK).transpose(1, 0, 2)
    return pl.pallas_call(
        moments_kernel,
        grid=(steps,),
        in_specs=[
            row_spec(cells),
            pl.BlockSpec((1, height, ROW_BLOCK), lambda i: (i, 0, 0)),
        ],
        out_specs=full_spec((height, cells)),
        out_shape=jax.ShapeDtypeStruct((height, cells), jnp.float32),
        compiler_params=pltpu.CompilerParams(dimension_semantics=("arbitrary",)),
        cost_estimate=pl.CostEstimate(
            flops=2 * rows * cells * height,
            bytes_accessed=rows * cells * 2 + height * cells * 4,
            transcendentals=0,
        ),
    )(dist, blocks)


def stencil_moments(dist, left, right, courant, basis):
    ahead = jnp.maximum(courant[:, 0], 0.0)
    behind = jnp.minimum(courant[:, 0], 0.0)
    weights = basis.astype(jnp.float32)
    stencil = [weights * (1.0 - ahead + behind)[None, :], weights * ahead[None, :], -weights * behind[None, :]]
    stacked = split_three(jnp.concatenate(stencil, axis=0))
    products = moments_call(dist, stacked)
    parts = products.reshape(3, 3, MOMENTS, dist.shape[1])
    parts = (parts[0] + parts[1]) + parts[2]
    edge_left = jnp.sum(stencil[1] * left[:, 0].astype(jnp.float32)[None, :], axis=1)
    edge_right = jnp.sum(stencil[2] * right[:, 0].astype(jnp.float32)[None, :], axis=1)
    from_left = jnp.concatenate([edge_left[:, None], parts[1][:, :-1]], axis=1)
    from_right = jnp.concatenate([parts[2][:, 1:], edge_right[:, None]], axis=1)
    return (parts[0] + from_left) + from_right


def relax_call(dist, left, right, courant, recon3, gain, keep):
    rows, cells = dist.shape
    steps = rows // ROW_BLOCK
    return pl.pallas_call(
        relax_kernel,
        grid=(steps,),
        in_specs=[
            row_spec(cells),
            row_spec(1),
            row_spec(1),
            row_spec(1),
            row_spec(recon3.shape[1]),
            full_spec(gain.shape),
            full_spec(keep.shape),
        ],
        out_specs=row_spec(cells),
        out_shape=jax.ShapeDtypeStruct((rows, cells), jnp.bfloat16),
        scratch_shapes=[pltpu.VMEM((ROW_BLOCK, cells), jnp.float32)],
        compiler_params=pltpu.CompilerParams(dimension_semantics=("parallel",)),
        cost_estimate=pl.CostEstimate(
            flops=2 * rows * cells * 60 + 10 * rows * cells,
            bytes_accessed=rows * cells * 4,
            transcendentals=0,
        ),
    )(dist, left, right, courant, recon3, gain, keep)


def split_three(values):
    first = lax.reduce_precision(values, exponent_bits=8, mantissa_bits=7)
    rest = values - first
    second = lax.reduce_precision(rest, exponent_bits=8, mantissa_bits=7)
    third = rest - second
    parts = [first, second, third]
    return jnp.concatenate([part.astype(jnp.bfloat16) for part in parts], axis=0)


def sect_sum(values):
    count = lax.axis_size("sect")
    total = values
    step = 1
    while step < count:
        pairs = [(i, i ^ step) for i in range(count)]
        total = total + lax.ppermute(total, "sect", pairs)
        step *= 2
    return total


def interface_rows(plenum_moments, iface_cell, width, base):
    count = lax.axis_size("sect")
    share = plenum_moments.shape[0] // count
    start = lax.axis_index("sect") * share
    coded = jnp.concatenate(
        [
            plenum_moments.astype(jnp.bfloat16),
            (iface_cell // 256).astype(jnp.bfloat16)[:, None],
            (iface_cell % 256).astype(jnp.bfloat16)[:, None],
        ],
        axis=1,
    )
    coded = lax.dynamic_slice_in_dim(coded, start, share, axis=0)
    peers = lax.axis_size("space")
    spread_out = jnp.broadcast_to(coded[None], (peers,) + coded.shape).reshape(peers * share, -1)
    gathered = lax.all_to_all(spread_out, "space", 0, 0, tiled=True)
    return fold_interface(gathered, width, base)


def fold_interface(gathered, width, base):
    low = width // CELL_HI
    rows = gathered[:, :MOMENTS]
    cells = gathered[:, MOMENTS].astype(jnp.int32) * 256 + gathered[:, MOMENTS + 1].astype(jnp.int32)
    local = cells - base
    valid = (local >= 0) & (local < width)
    upper = jnp.where(valid, local // low, -1)
    lower = local % low
    extended = jnp.concatenate([rows, jnp.ones((rows.shape[0], 1), jnp.bfloat16)], axis=1)
    pick_hi = (upper[:, None] == jnp.arange(CELL_HI, dtype=jnp.int32)[None, :]).astype(jnp.bfloat16)
    spread = (pick_hi[:, :, None] * extended[:, None, :]).reshape(rows.shape[0], -1)
    pick_lo = (lower[:, None] == jnp.arange(low, dtype=jnp.int32)[None, :]).astype(jnp.bfloat16)
    folded = lax.dot_general(
        spread, pick_lo, (((0,), (0,)), ((), ())), preferred_element_type=jnp.float32
    )
    return folded.reshape(CELL_HI, MOMENTS + 1, low).transpose(1, 0, 2).reshape(MOMENTS + 1, width)


def inject(closure, folded):
    fluid = folded[:MOMENTS]
    hit = folded[MOMENTS]
    return closure + hit[None, :] * (fluid - closure)


def ghost_tables(cells, ghost_source, ghost_owner, wall_cell):
    peers = lax.axis_size("space")
    capacity = wall_cell.shape[2]
    slots = peers * capacity
    owner = ghost_owner[:, 0]
    marks = (owner[:, None] == jnp.arange(peers, dtype=jnp.int32)[None, :]).astype(jnp.int32)
    before = jnp.cumsum(marks, axis=0) - marks
    slot = jnp.sum(marks * before, axis=1)
    places = owner * capacity + slot
    at_place = (places[:, None] == jnp.arange(slots, dtype=jnp.int32)[None, :]).astype(jnp.int32)
    source_of = jnp.sum(at_place * (ghost_source[:, None] + 1), axis=0) - 1
    select = (jnp.arange(cells, dtype=jnp.int32)[:, None] == source_of[None, :]).astype(jnp.bfloat16)
    walls = wall_cell.reshape(slots)
    land = (walls[:, None] == jnp.arange(cells, dtype=jnp.int32)[None, :]).astype(jnp.bfloat16)
    return select, land


def ghost_walls(targets, select, land):
    outgoing = jnp.dot(targets, select, preferred_element_type=jnp.float32).astype(jnp.bfloat16)
    arrived = lax.all_to_all(outgoing, "space", split_axis=1, concat_axis=1, tiled=True)
    return jnp.dot(arrived, land, preferred_element_type=jnp.float32)


def per_device(
    dist,
    velocity,
    quad_weight,
    collision_rate,
    ghost_source,
    ghost_owner,
    wall_cell,
    plenum_moments,
    iface_cell,
):
    cells = dist.shape[1]
    courant = (COURANT_SCALE * velocity[0])[:, None]
    left, right = halo_columns(dist)
    partial_moments = stencil_moments(
        dist, left, right, courant, moment_basis(velocity, quad_weight)
    )
    slab_base = lax.axis_index("space") * cells
    select, land = ghost_tables(cells, ghost_source, ghost_owner, wall_cell)
    select, land = lax.optimization_barrier((select, land))
    recon = recon_basis(velocity)
    recon3 = lax.optimization_barrier(jnp.concatenate([recon, recon, recon], axis=1))
    moments = sect_sum(partial_moments)
    partial_rows = interface_rows(plenum_moments, iface_cell, cells, slab_base)
    rows = sect_sum(partial_rows.astype(jnp.bfloat16)).astype(jnp.float32)
    targets = inject(es_targets(moments), rows).astype(jnp.bfloat16)
    wall_moments = ghost_walls(targets, select, land)
    rate = collision_rate[None, :]
    gain = split_three(rate * targets.astype(jnp.float32) + WALL_SHARE * wall_moments)
    return relax_call(dist, left, right, courant, recon3, gain, 1.0 - rate)


def solution(mesh):
    in_specs = (
        P("sect", "space"),
        P(None, "sect"),
        P("sect"),
        P("space"),
        P("space"),
        P("space", None),
        P("space", None, None),
        P("space", None),
        P("space"),
    )
    out_specs = P("sect", "space")

    return jax.shard_map(per_device, mesh=mesh, in_specs=in_specs, out_specs=out_specs, check_vma=False)
```

```python
import jax
import jax.numpy as jnp
from jax import lax
from jax.experimental import pallas as pl
from jax.experimental.pallas import tpu as pltpu
from jax.sharding import PartitionSpec as P


NV = 8000
MOMENTS = 20


COURANT_SCALE = 0.6
ES_SHIFT = -0.5
WALL_SHARE = 0.5
ORDER_TWO = ((0, 0), (1, 1), (2, 2), (0, 1), (0, 2), (1, 2))
ORDER_THREE = (
    (0, 0, 0),
    (1, 1, 1),
    (2, 2, 2),
    (0, 0, 1),
    (0, 0, 2),
    (1, 1, 0),
    (1, 1, 2),
    (2, 2, 0),
    (2, 2, 1),
    (0, 1, 2),
)
RECON_NORMS = (
    1.0,
    1.0,
    1.0,
    1.0,
    2.0,
    2.0,
    2.0,
    1.0,
    1.0,
    1.0,
    6.0,
    6.0,
    6.0,
    2.0,
    2.0,
    2.0,
    2.0,
    2.0,
    2.0,
    1.0,
)
ROW_BLOCK = 400
CHUNK = 16
CELL_HI = 8


def halo_columns(shard):
    count = lax.axis_size("space")
    length = shard.shape[1]
    up = [(i, i + 1) for i in range(count - 1)]
    down = [(j, i) for i, j in up]
    before = lax.ppermute(shard[:, length - 1], "space", up)
    after = lax.ppermute(shard[:, 0], "space", down)
    return before[:, None], after[:, None]


def hermite_tables():
    factors = [[0, 0, 0]]
    corrections = [[4, 4, 4]]
    for i in range(3):
        factors.append([i + 1, 0, 0])
        corrections.append([4, 4, 4])
    for i, j in ORDER_TWO:
        factors.append([i + 1, j + 1, 0])
        corrections.append([0 if i == j else 4, 4, 4])
    for i, j, k in ORDER_THREE:
        factors.append([i + 1, j + 1, k + 1])
        corrections.append(
            [k + 1 if i == j else 4, j + 1 if i == k else 4, i + 1 if j == k else 4]
        )
    return factors, corrections


def hermite(velocity):
    factors, corrections = hermite_tables()
    width = velocity.shape[1]
    extended = jnp.concatenate(
        [jnp.ones((1, width), jnp.float32), velocity, jnp.zeros((1, width), jnp.float32)], axis=0
    )

    def pick(column):
        chosen = jnp.array(column, dtype=jnp.int32)
        total = None
        for m in range(5):
            term = (chosen == m).astype(jnp.float32)[:, None] * extended[m][None, :]
            total = term if total is None else total + term
        return total

    first, second, third = [pick([f[n] for f in factors]) for n in range(3)]
    element = first * second * third
    for n in range(3):
        element = element - pick([c[n] for c in corrections])
    return element


def moment_basis(velocity, weight):
    return (hermite(velocity) * (weight / NV)[None, :]).astype(jnp.bfloat16)


def recon_basis(velocity):
    norms = jnp.array(RECON_NORMS, dtype=jnp.float32)
    return (hermite(velocity) / norms[:, None]).T.astype(jnp.bfloat16)


def es_targets(moments):
    density = moments[0]
    moving = [moments[1], moments[2], moments[3]]
    trace_sum = moments[4] + moments[5] + moments[6]
    second = [[None, None, None], [None, None, None], [None, None, None]]
    for n, (i, j) in enumerate(ORDER_TWO):
        element = (1.0 - ES_SHIFT) * moments[4 + n]
        if i == j:
            element = element + ES_SHIFT * trace_sum / 3.0
        second[i][j] = element
        second[j][i] = element
    stacked = [density] + moving + [second[i][j] for i, j in ORDER_TWO]
    for n, (i, j, k) in enumerate(ORDER_THREE):
        stacked.append(
            0.5 * moments[10 + n]
            + (moving[i] * second[j][k] + moving[j] * second[i][k] + moving[k] * second[i][j])
            / density
        )
    return jnp.stack(stacked)


def transport_block(dist_ref, left_ref, right_ref, courant_ref):
    centre = dist_ref[...].astype(jnp.float32)
    width = centre.shape[1]
    column = lax.broadcasted_iota(jnp.int32, (1, width), 1)
    left = jnp.where(
        column == 0, left_ref[...].astype(jnp.float32), pltpu.roll(centre, 1, 1)
    )
    right = jnp.where(
        column == width - 1,
        right_ref[...].astype(jnp.float32),
        pltpu.roll(centre, width - 1, 1),
    )
    courant = courant_ref[...]
    ahead = jnp.maximum(courant, 0.0)
    behind = jnp.minimum(courant, 0.0)
    return (centre - ahead * (centre - left) - behind * (right - centre)).astype(jnp.bfloat16)


def moments_kernel(dist_ref, basis_ref, out_ref):
    @pl.when(pl.program_id(0) == 0)
    def _():
        out_ref[...] = jnp.zeros_like(out_ref)

    out_ref[...] += jnp.dot(basis_ref[0], dist_ref[...], preferred_element_type=jnp.float32)


def relax_kernel(
    dist_ref, left_ref, right_ref, courant_ref, recon3_ref, gain_ref, keep_ref, out_ref, gained_ref,
):
    gained_ref[...] = jnp.dot(recon3_ref[...], gain_ref[...], preferred_element_type=jnp.float32)
    keep = keep_ref[...]

    def chunk(step, carry):
        rows = pl.ds(pl.multiple_of(step * CHUNK, CHUNK), CHUNK)
        read = transport_block(
            dist_ref.at[rows], left_ref.at[rows], right_ref.at[rows], courant_ref.at[rows]
        ).astype(jnp.float32)
        out_ref[rows, :] = (read * keep + gained_ref[rows, :]).astype(out_ref.dtype)
        return carry

    lax.fori_loop(0, ROW_BLOCK // CHUNK, chunk, 0, unroll=True)


def row_spec(width):
    return pl.BlockSpec((ROW_BLOCK, width), lambda i: (i, 0))


def full_spec(shape):
    return pl.BlockSpec(shape, lambda i: (0,) * len(shape))


def moments_call(dist, basis):
    rows, cells = dist.shape
    steps = rows // ROW_BLOCK
    height = basis.shape[0]
    blocks = basis.reshape(height, steps, ROW_BLOCK).transpose(1, 0, 2)
    return pl.pallas_call(
        moments_kernel,
        grid=(steps,),
        in_specs=[
            row_spec(cells),
            pl.BlockSpec((1, height, ROW_BLOCK), lambda i: (i, 0, 0)),
        ],
        out_specs=full_spec((height, cells)),
        out_shape=jax.ShapeDtypeStruct((height, cells), jnp.float32),
        compiler_params=pltpu.CompilerParams(dimension_semantics=("arbitrary",)),
        cost_estimate=pl.CostEstimate(
            flops=2 * rows * cells * height,
            bytes_accessed=rows * cells * 2 + height * cells * 4,
            transcendentals=0,
        ),
    )(dist, blocks)


def stencil_moments(dist, left, right, courant, basis):
    ahead = jnp.maximum(courant[:, 0], 0.0)
    behind = jnp.minimum(courant[:, 0], 0.0)
    weights = basis.astype(jnp.float32)
    stencil = [weights * (1.0 - ahead + behind)[None, :], weights * ahead[None, :], -weights * behind[None, :]]
    stacked = split_three(jnp.concatenate(stencil, axis=0))
    products = moments_call(dist, stacked)
    parts = products.reshape(3, 3, MOMENTS, dist.shape[1])
    parts = (parts[0] + parts[1]) + parts[2]
    edge_left = jnp.sum(stencil[1] * left[:, 0].astype(jnp.float32)[None, :], axis=1)
    edge_right = jnp.sum(stencil[2] * right[:, 0].astype(jnp.float32)[None, :], axis=1)
    from_left = jnp.concatenate([edge_left[:, None], parts[1][:, :-1]], axis=1)
    from_right = jnp.concatenate([parts[2][:, 1:], edge_right[:, None]], axis=1)
    return (parts[0] + from_left) + from_right


def relax_call(dist, left, right, courant, recon3, gain, keep):
    rows, cells = dist.shape
    steps = rows // ROW_BLOCK
    return pl.pallas_call(
        relax_kernel,
        grid=(steps,),
        in_specs=[
            row_spec(cells),
            row_spec(1),
            row_spec(1),
            row_spec(1),
            row_spec(recon3.shape[1]),
            full_spec(gain.shape),
            full_spec(keep.shape),
        ],
        out_specs=row_spec(cells),
        out_shape=jax.ShapeDtypeStruct((rows, cells), jnp.bfloat16),
        scratch_shapes=[pltpu.VMEM((ROW_BLOCK, cells), jnp.float32)],
        compiler_params=pltpu.CompilerParams(dimension_semantics=("parallel",)),
        cost_estimate=pl.CostEstimate(
            flops=2 * rows * cells * 60 + 10 * rows * cells,
            bytes_accessed=rows * cells * 4,
            transcendentals=0,
        ),
    )(dist, left, right, courant, recon3, gain, keep)


def split_three(values):
    first = lax.reduce_precision(values, exponent_bits=8, mantissa_bits=7)
    rest = values - first
    second = lax.reduce_precision(rest, exponent_bits=8, mantissa_bits=7)
    third = rest - second
    parts = [first, second, third]
    return jnp.concatenate([part.astype(jnp.bfloat16) for part in parts], axis=0)


def sect_sum(values):
    count = lax.axis_size("sect")
    total = values
    step = 1
    while step < count:
        pairs = [(i, i ^ step) for i in range(count)]
        total = total + lax.ppermute(total, "sect", pairs)
        step *= 2
    return total


def interface_rows(plenum_moments, iface_cell, width, base):
    count = lax.axis_size("sect")
    share = plenum_moments.shape[0] // count
    start = lax.axis_index("sect") * share
    coded = jnp.concatenate(
        [
            plenum_moments.astype(jnp.bfloat16),
            (iface_cell // 256).astype(jnp.bfloat16)[:, None],
            (iface_cell % 256).astype(jnp.bfloat16)[:, None],
        ],
        axis=1,
    )
    coded = lax.dynamic_slice_in_dim(coded, start, share, axis=0)
    peers = lax.axis_size("space")
    spread_out = jnp.broadcast_to(coded[None], (peers,) + coded.shape).reshape(peers * share, -1)
    gathered = lax.all_to_all(spread_out, "space", 0, 0, tiled=True)
    return fold_interface(gathered, width, base)


def fold_interface(gathered, width, base):
    low = width // CELL_HI
    rows = gathered[:, :MOMENTS]
    cells = gathered[:, MOMENTS].astype(jnp.int32) * 256 + gathered[:, MOMENTS + 1].astype(jnp.int32)
    local = cells - base
    valid = (local >= 0) & (local < width)
    upper = jnp.where(valid, local // low, -1)
    lower = local % low
    extended = jnp.concatenate([rows, jnp.ones((rows.shape[0], 1), jnp.bfloat16)], axis=1)
    pick_hi = (upper[:, None] == jnp.arange(CELL_HI, dtype=jnp.int32)[None, :]).astype(jnp.bfloat16)
    spread = (pick_hi[:, :, None] * extended[:, None, :]).reshape(rows.shape[0], -1)
    pick_lo = (lower[:, None] == jnp.arange(low, dtype=jnp.int32)[None, :]).astype(jnp.bfloat16)
    folded = lax.dot_general(
        spread, pick_lo, (((0,), (0,)), ((), ())), preferred_element_type=jnp.float32
    )
    return folded.reshape(CELL_HI, MOMENTS + 1, low).transpose(1, 0, 2).reshape(MOMENTS + 1, width)


def inject(closure, folded):
    fluid = folded[:MOMENTS]
    hit = folded[MOMENTS]
    return closure + hit[None, :] * (fluid - closure)


def ghost_tables(cells, ghost_source, ghost_owner, wall_cell):
    peers = lax.axis_size("space")
    capacity = wall_cell.shape[2]
    slots = peers * capacity
    owner = ghost_owner[:, 0]
    marks = (owner[:, None] == jnp.arange(peers, dtype=jnp.int32)[None, :]).astype(jnp.int32)
    before = jnp.cumsum(marks, axis=0) - marks
    slot = jnp.sum(marks * before, axis=1)
    places = owner * capacity + slot
    at_place = (places[:, None] == jnp.arange(slots, dtype=jnp.int32)[None, :]).astype(jnp.int32)
    source_of = jnp.sum(at_place * (ghost_source[:, None] + 1), axis=0) - 1
    select = (jnp.arange(cells, dtype=jnp.int32)[:, None] == source_of[None, :]).astype(jnp.bfloat16)
    walls = wall_cell.reshape(slots)
    land = (walls[:, None] == jnp.arange(cells, dtype=jnp.int32)[None, :]).astype(jnp.bfloat16)
    return select, land


def ghost_walls(targets, select, land):
    outgoing = jnp.dot(targets, select, preferred_element_type=jnp.float32).astype(jnp.bfloat16)
    arrived = lax.all_to_all(outgoing, "space", split_axis=1, concat_axis=1, tiled=True)
    return jnp.dot(arrived, land, preferred_element_type=jnp.float32)


def per_device(
    dist,
    velocity,
    quad_weight,
    collision_rate,
    ghost_source,
    ghost_owner,
    wall_cell,
    plenum_moments,
    iface_cell,
):
    cells = dist.shape[1]
    courant = (COURANT_SCALE * velocity[0])[:, None]
    left, right = halo_columns(dist)
    partial_moments = stencil_moments(
        dist, left, right, courant, moment_basis(velocity, quad_weight)
    )
    slab_base = lax.axis_index("space") * cells
    select, land = ghost_tables(cells, ghost_source, ghost_owner, wall_cell)
    select, land = lax.optimization_barrier((select, land))
    recon = recon_basis(velocity)
    recon3 = lax.optimization_barrier(jnp.concatenate([recon, recon, recon], axis=1))
    moments = sect_sum(partial_moments)
    partial_rows = interface_rows(plenum_moments, iface_cell, cells, slab_base)
    rows = sect_sum(partial_rows.astype(jnp.bfloat16)).astype(jnp.float32)
    targets = inject(es_targets(moments), rows).astype(jnp.bfloat16)
    wall_moments = ghost_walls(targets, select, land)
    rate = collision_rate[None, :]
    gain = split_three(rate * targets.astype(jnp.float32) + WALL_SHARE * wall_moments)
    return relax_call(dist, left, right, courant, recon3, gain, 1.0 - rate)


def solution(mesh):
    in_specs = (
        P("sect", "space"),
        P(None, "sect"),
        P("sect"),
        P("space"),
        P("space"),
        P("space", None),
        P("space", None, None),
        P("space", None),
        P("space"),
    )
    out_specs = P("sect", "space")

    return jax.shard_map(per_device, mesh=mesh, in_specs=in_specs, out_specs=out_specs, check_vma=False)
```
